1024 devices in a mesh: expert: 32 (over x, y, core), chan: 32 (over z).
Axes of the slice: x: 4, y: 4, z: 32, core: 2. Of those that a mesh axis runs over, the one named last changes fastest.
Arguments:
- tiles_in: bfloat16 [1024, 3, 3, 2048], P('expert', None, None, 'chan'), may hold values from -6 to 6
- grad_out: bfloat16 [1024, 3, 3, 2048], P('expert', None, None, 'chan'), may hold values from -6 to 6
- gate: bfloat16 [1024], P('expert'), may hold values from 0.19921875 to 1
- expert_id: int32 [1024, 1], P('expert'), may hold values from 0 to 31; in each aligned block of 32 rows (0 to 31, 32 to 63, ...) at most 2 rows name the same one
- w_conv: bfloat16 [32, 3, 3, 32, 16384], P('expert', None, None, None, 'chan'), may hold values from -0.375 to 0.375
- w_depth: bfloat16 [32, 9, 16384], P('expert', None, 'chan'), may hold values from -2 to 2
- w_out: bfloat16 [32, 16384, 2048], P('expert', 'chan'), may hold values from -0.046875 to 0.046875
Outputs:
- grad_input: bfloat16 [1024, 3, 3, 2048], P('expert', None, None, 'chan')
- grad_gate: bfloat16 [1024], P('expert')
The draws below stay inside these ranges and needn't reach their ends.
Inputs may be any that keep to these rules, and one draw needn't show every extreme that they name: `expert_id`: within the 32 tiles of one index of expert, no expert is named more than 2 times, and in every draw some expert is named exactly 2 times there.
All inputs are finite; a program needn't handle non-finite values.
Results may differ from the reference program's by a relative error of at most 0.009.
Values may be sent and summed in bfloat16 or wider, within the bound.
No kernel may reach another device: no remote copies, remote signals or barrier semaphores. Data moves between devices by JAX's collectives and lax.ppermute only.
A program may use at most 32 MiB of HBM per device.

```python
import math
import jax
import jax.numpy as jnp
import numpy as np
from jax import lax

D = 2048
F = 16384
GROUPS = 64
TS = 3
CAP = 2
TILES_DEV = 32
EXPERTS = 32
TILES = 1024
DG = 32
N_EXPERT = 32


def levels(own_key, dims, cuts, smallest, largest):
    factor_of, own = 1.0, jax.random.fold_in(own_key, 6)
    for dim, blocks in cuts:
        heights = jnp.exp(jax.random.uniform(jax.random.fold_in(own, dim), (blocks,), jnp.float32, smallest / len(cuts), largest / len(cuts)))
        factor_of = factor_of * jnp.repeat(heights, dims[dim] // blocks).reshape([-1 if axis == dim else 1 for axis in range(len(dims))])
    return factor_of


def deal_out(stream_key, own, number, rows, count, top, limit, slope):
    order = jax.random.permutation(stream_key, count)
    heavy_load, common = load_shares(count, rows * top, limit, slope, True), load_shares(count, rows * top, limit, slope, False)
    places = jnp.arange(count)

    def named(lengths, turn):
        used = int((lengths > 0).sum())
        fixed = max(1, used // 4)
        passed = fixed + (places - fixed + turn * (used - fixed)) % max(1, count - fixed)
        return jnp.zeros((count,), jnp.int32).at[order[jnp.where(places < fixed, places, passed)]].set(jnp.asarray(lengths, jnp.int32))

    lengths = jnp.where(number % 4 == 0, named(heavy_load, number // 4), named(common, number - number // 4 - 1))
    mixed = jax.random.permutation(jax.random.fold_in(own, 3), count)
    source_of, taker = mixed[0:count // 2 * 2:2], mixed[1:count // 2 * 2:2]
    margin = jnp.minimum(lengths[source_of] - 1, limit - lengths[taker]) // 2
    margin = jnp.where((source_of == order[0]) | (taker == order[0]) | (lengths[taker] == 0), 0, jnp.maximum(margin, 0))
    passed = jax.random.randint(jax.random.fold_in(own, 4), (count // 2,), 0, 1 << 20) % (margin + 1)
    lengths = lengths.at[source_of].add(-passed).at[taker].add(passed)
    members = jnp.searchsorted(jnp.cumsum(lengths), jnp.arange(rows * top), side="right").astype(jnp.int32)
    table = members.reshape(top, rows).T
    table = table[jax.random.permutation(jax.random.fold_in(own, 1), rows)]
    turn = jax.random.randint(jax.random.fold_in(own, 2), (rows, 1), 0, top)
    return jnp.take_along_axis(table, (jnp.arange(top)[None, :] + turn) % top, axis=1)


def load_shares(number_of, total, most, skew, full):
    weights = [(1 << 20) // math.isqrt(standing ** skew) + 1 for standing in range(1, number_of + 1)]
    largest = most if full else min(most, max(-(-total // number_of), total * weights[0] // sum(weights)))
    least = 1 if total - largest >= number_of - 1 else 0
    counts, surplus = [largest] + [least] * (number_of - 1), total - largest - least * (number_of - 1)
    while surplus > 0:
        candidates = [i for i in range(1, number_of) if counts[i] < largest] or [i for i in range(1, number_of) if counts[i] < most]
        mass, budget = sum([weights[i] for i in candidates]), surplus
        for i in candidates:
            addition = min(most - counts[i], max(1, budget * weights[i] // mass), surplus)
            counts[i] = counts[i] + addition
            surplus = surplus - addition
    return np.array(counts)


def gaussian(rng, dims, width, most, shards=(), kind=jnp.bfloat16):
    array = width * jax.random.normal(rng, dims, jnp.float32)
    if shards:
        array = array * levels(rng, dims, shards, -0.22, 0.18)
    return jnp.clip(array, -most, most).astype(kind)


def setup_inputs(seed: int = 0) -> dict:
    streams_of = jax.random.split(jax.random.key(seed), 8)
    tiles_in = gaussian(streams_of[0], (TILES, TS, TS, D), 1.0, 6.0, ((0, 32), (3, 32)))
    grad_out = gaussian(streams_of[1], (TILES, TS, TS, D), 1.0, 6.0, ((0, 32), (3, 32)))
    gate = jnp.clip(jnp.exp(math.log(1.0) - 1.6133518 * jax.random.uniform(streams_of[2], (TILES,), jnp.float32) ** levels(streams_of[2], (TILES,), ((0, 32),), -0.2, 0.2)), 0.19921875, 1.0).astype(jnp.bfloat16)
    expert_id_keys = jax.random.split(jax.random.fold_in(streams_of[3], 1), TILES // TILES_DEV)
    expert_id_turns = jax.random.permutation(jax.random.fold_in(streams_of[3], 3), TILES // TILES_DEV)
    expert_id = jax.vmap(lambda own, number: deal_out(jax.random.fold_in(streams_of[3], 2), own, number, TILES_DEV, EXPERTS, 1, CAP, 2))(expert_id_keys, expert_id_turns).reshape((TILES, 1))
    w_conv = gaussian(streams_of[4], (EXPERTS, 3, 3, DG, F), (9 * DG) ** -0.5, 0.375, ((0, 32), (4, 32)))
    w_depth = gaussian(streams_of[5], (EXPERTS, 9, F), 9 ** -0.5, 2.0, ((0, 32), (2, 32)))
    w_out = gaussian(streams_of[6], (EXPERTS, F, D), F ** -0.5, 0.046875, ((0, 32), (1, 32)))
    return {"tiles_in": tiles_in, "grad_out": grad_out, "gate": gate, "expert_id": expert_id, "w_conv": w_conv, "w_depth": w_depth, "w_out": w_out}


def group_conv(field, kernel, count):
    return lax.conv_general_dilated(field, kernel, (1, 1), 'SAME', dimension_numbers=('NHWC', 'HWIO', 'NHWC'), feature_group_count=count, preferred_element_type=jnp.float32)

def conv_back(field, kernel, count, cotangent):
    forward_value, pullback = jax.vjp(lambda value: group_conv(value, kernel, count), field)
    return pullback(cotangent)[0]

def gelu_slope(value):
    normal_cdf = 0.5 * (1.0 + jax.scipy.special.erf(value * 0.7071067811865476))
    return normal_cdf + value * jnp.exp(-0.5 * value * value) * 0.3989422804014327

def depth_forward(field, taps):
    side = field.shape[1]
    padded = jnp.pad(field, ((0, 0), (1, 1), (1, 1), (0, 0))).astype(jnp.float32)
    total = jnp.zeros(field.shape, jnp.float32)
    for row_off in range(3):
        for col_off in range(3):
            total = total + padded[:, row_off:row_off + side, col_off:col_off + side, :] * taps[3 * row_off + col_off].astype(jnp.float32)
    return total

def depth_back(field, taps):
    side = field.shape[1]
    padded = jnp.pad(field, ((0, 0), (1, 1), (1, 1), (0, 0))).astype(jnp.float32)
    total = jnp.zeros(field.shape, jnp.float32)
    for row_off in range(3):
        for col_off in range(3):
            total = total + padded[:, 2 - row_off:2 - row_off + side, 2 - col_off:2 - col_off + side, :] * taps[3 * row_off + col_off].astype(jnp.float32)
    return total

def one_expert(items):
    inputs, grads, gates, kernel, taps, project = items
    slots = inputs.shape[0]
    h_one = group_conv(inputs, kernel, GROUPS)
    active = jax.nn.gelu(h_one, approximate=False).astype(jnp.bfloat16)
    h_two = depth_forward(active, taps).astype(jnp.bfloat16)
    upper = jnp.dot(grads.reshape(-1, D).astype(jnp.float32), project.astype(jnp.float32).T)
    upper = upper.reshape(slots, TS, TS, F)
    gate_grad = lax.optimization_barrier(jnp.sum(h_two.astype(jnp.float32) * upper, axis=(1, 2, 3)))
    d_two = (gates.astype(jnp.float32)[:, None, None, None] * upper).astype(jnp.bfloat16)
    d_act = depth_back(d_two, taps)
    d_one = (d_act * gelu_slope(h_one)).astype(jnp.bfloat16)
    d_input = conv_back(inputs, kernel, GROUPS, d_one.astype(jnp.float32))
    return (d_input.astype(jnp.bfloat16), gate_grad.astype(jnp.bfloat16))

def reference(tiles_in, grad_out, gate, expert_id, w_conv, w_depth, w_out):
    chosen = expert_id[:, 0].astype(jnp.int32)
    matches = (chosen[:, None] == jnp.arange(EXPERTS, dtype=jnp.int32)[None, :]).astype(jnp.int32)
    blocked = matches.reshape(N_EXPERT, TILES_DEV, EXPERTS)
    before = jnp.cumsum(blocked, axis=1) - blocked
    rank = lax.optimization_barrier(jnp.sum(before * blocked, axis=2)).reshape(TILES)
    source = jnp.arange(TILES, dtype=jnp.int32) // TILES_DEV
    slot = (source * CAP + rank).astype(jnp.int32)
    slots = N_EXPERT * CAP
    input_buf = jnp.zeros((EXPERTS, slots, TS, TS, D), jnp.bfloat16).at[chosen, slot].set(tiles_in)
    grad_buf = jnp.zeros((EXPERTS, slots, TS, TS, D), jnp.bfloat16).at[chosen, slot].set(grad_out)
    gate_buf = jnp.zeros((EXPERTS, slots), jnp.bfloat16).at[chosen, slot].set(gate)
    taps = w_depth
    d_buf, g_buf = lax.map(one_expert, (input_buf, grad_buf, gate_buf, w_conv, taps, w_out))
    return (d_buf[chosen, slot], g_buf[chosen, slot])
```

```python
import jax
import jax.numpy as jnp
from jax import lax
from jax.experimental import pallas as pl
from jax.experimental.pallas import tpu as pltpu
from jax.sharding import PartitionSpec as P

CAP = 2


def near(pos, off, side):
    row, col = pos // side + off // 3 - 1, pos % side + off % 3 - 1
    return row * side + col if 0 <= row < side and 0 <= col < side else None


def project_kernel(feat_ref, weight_ref, h_two_ref, gate_ref, d_two_ref, part_ref, left_ref):
    blocks, rows, lanes = feat_ref.shape
    half = lanes // 2
    tokens, slots, hidden = d_two_ref.shape
    own = slots // 2
    for block in range(0, blocks, 2):
        first = feat_ref[block]
        second = feat_ref[block + 1]
        span = slice(block * half, (block + 2) * half)
        left_ref[:rows, span] = jnp.concatenate([first[:, :half], second[:, :half]], axis=1)
        left_ref[rows:, span] = jnp.concatenate([first[:, half:], second[:, half:]], axis=1)
    wide = 256
    for group in range(2):
        keep = slice(group * own, (group + 1) * own)
        scale = gate_ref[keep, :][:, :1]
        total = jnp.zeros((own, 128), jnp.float32)
        for start in range(0, hidden, wide):
            upper = lax.dot_general(
                left_ref[group * rows : (group + 1) * rows, :],
                weight_ref[start : start + wide, :],
                (((1,), (1,)), ((), ())),
                preferred_element_type=jnp.float32,
            )
            for pos in range(tokens):
                piece = upper[pos * own : (pos + 1) * own, :]
                d_two_ref[pos, keep, start : start + wide] = (piece * scale).astype(jnp.bfloat16)
                prod = h_two_ref[pos, keep, start : start + wide].astype(jnp.float32) * piece
                for lane in range(0, wide, 128):
                    total = total + prod[:, lane : lane + 128]
        part_ref[keep, :] = total


def back_kernel(d_two_ref, slope_ref, taps_ref, kernel_ref, d_in_ref, d_one_ref, *, side):
    tokens, slots, hidden = d_two_ref.shape
    wide = 256
    for start in range(0, hidden, wide):
        span = slice(start, start + wide)
        for pos in range(tokens):
            total = jnp.zeros((slots, wide), jnp.float32)
            for off in range(9):
                other = near(pos, 8 - off, side)
                if other is not None:
                    total = total + d_two_ref[other, :, span].astype(jnp.float32) * taps_ref[
                        off : off + 1, span
                    ].astype(jnp.float32)
            d_one_ref[pos, :, span] = (total * slope_ref[pos, :, span]).astype(jnp.bfloat16)
    for pos in range(tokens):
        total = jnp.zeros(d_in_ref.shape[1:], jnp.float32)
        for off in range(9):
            other = near(pos, 8 - off, side)
            if other is not None:
                total = total + lax.dot_general(
                    d_one_ref[other],
                    kernel_ref[off],
                    (((1,), (1,)), ((), ())),
                    preferred_element_type=jnp.float32,
                )
        d_in_ref[pos] = total.astype(jnp.bfloat16)


def vmem(count):
    return [pl.BlockSpec(memory_space=pltpu.VMEM) for _ in range(count)]


def forward(inputs, kernel, taps, side):
    tokens = side * side
    blank = jnp.zeros_like(inputs[0])
    columns = []
    for pos in range(tokens):
        picked = [near(pos, off, side) for off in range(9)]
        columns.append(
            jnp.concatenate([blank if n is None else inputs[n] for n in picked], axis=1)
        )
    h_one = jnp.einsum(
        "psk,kf->psf",
        jnp.stack(columns),
        kernel.reshape(-1, kernel.shape[2]),
        preferred_element_type=jnp.float32,
    )
    active = jax.nn.gelu(h_one, approximate=False).astype(jnp.bfloat16)
    grid = active.reshape(side, side, *active.shape[1:])
    padded = jnp.pad(grid, ((1, 1), (1, 1), (0, 0), (0, 0))).astype(jnp.float32)
    total = jnp.zeros(grid.shape, jnp.float32)
    for row in range(3):
        for col in range(3):
            total = total + padded[row : row + side, col : col + side] * taps[3 * row + col].astype(
                jnp.float32
            )
    h_two = total.reshape(active.shape).astype(jnp.bfloat16)
    cdf = 0.5 * (1.0 + lax.erf(h_one * 0.7071067811865476))
    slope = cdf + h_one * jnp.exp(-0.5 * h_one * h_one) * 0.3989422804014327
    return h_two, slope


def on_device(tiles_in, grad_out, gate, expert_id, w_conv, w_depth, w_out):
    owned, side, _, feat = tiles_in.shape
    tokens = side * side
    width = tokens * feat
    sections = lax.axis_size("expert")
    slots = sections * CAP
    hidden = w_out.shape[1]
    group = w_conv.shape[3]
    chosen = expert_id[:, 0]
    matches = (chosen[:, None] == jnp.arange(sections, dtype=jnp.int32)[None, :]).astype(jnp.int32)
    rows = jnp.arange(owned, dtype=jnp.int32)
    earlier = (rows[:, None] > rows[None, :]) & (chosen[:, None] == chosen[None, :])
    rank = jnp.sum(earlier.astype(jnp.int32), axis=1)
    slot = chosen * CAP + rank
    placing = (slot[:, None] == jnp.arange(slots, dtype=jnp.int32)[None, :]).astype(jnp.bfloat16)

    def place(array):
        out = lax.dot_general(
            placing, array, (((0,), (0,)), ((), ())), preferred_element_type=jnp.float32
        )
        return out.astype(jnp.bfloat16).reshape(sections, CAP, -1)

    def exchange(array):
        return lax.all_to_all(array, "expert", split_axis=0, concat_axis=0, tiled=True)

    tail = 64
    grads = exchange(place(grad_out.reshape(owned, width)))
    packed = grads.reshape(sections, CAP, tokens, feat).transpose(2, 0, 1, 3)
    packed = packed.reshape(tokens * sections, CAP * feat)
    extra = jnp.pad(gate[:, None], ((0, 0), (0, tail - 1)))
    outward = place(jnp.concatenate([tiles_in.reshape(owned, width), extra], axis=1))
    packed, outward = lax.optimization_barrier((packed, outward))
    gathered = lax.all_gather(packed, "chan", axis=0, tiled=False)
    arrived = exchange(outward)

    inputs = arrived[:, :, :width].reshape(sections, CAP, tokens, feat).transpose(2, 1, 0, 3)
    inputs = inputs.reshape(tokens, slots, feat)
    gates = arrived[:, :, width].T.reshape(slots, 1).astype(jnp.float32)
    gates = jnp.broadcast_to(gates, (slots, 128))
    taps = w_depth[0]
    small = w_conv[0].reshape(9, group, hidden)
    count = feat // group
    per = hidden // count
    which = jnp.arange(hidden, dtype=jnp.int32) // per
    kernel = jnp.concatenate(
        [jnp.where(which == g, small, jnp.zeros_like(small)) for g in range(count)], axis=1
    )
    h_two, slope = forward(inputs, kernel, taps, side)

    d_two, part = pl.pallas_call(
        project_kernel,
        out_shape=(
            jax.ShapeDtypeStruct((tokens, slots, hidden), jnp.bfloat16),
            jax.ShapeDtypeStruct((slots, 128), jnp.float32),
        ),
        in_specs=vmem(4),
        out_specs=tuple(vmem(2)),
        scratch_shapes=[
            pltpu.VMEM((tokens * slots, w_out.shape[2]), jnp.bfloat16),
        ],
        name="project",
    )(gathered, w_out[0], h_two, gates)
    part = jnp.sum(part, axis=1)
    part = jnp.pad(part, (0, 128 - slots))
    chans = lax.axis_size("chan")
    parts = lax.all_to_all(
        jnp.broadcast_to(part[None], (chans, 128)), "chan", split_axis=0, concat_axis=0, tiled=True
    )
    gate_grad = jnp.sum(parts, axis=0)[:slots].astype(jnp.bfloat16)
    d_input = pl.pallas_call(
        lambda *refs: back_kernel(*refs, side=side),
        out_shape=jax.ShapeDtypeStruct((tokens, slots, feat), jnp.bfloat16),
        in_specs=vmem(4),
        out_specs=vmem(1)[0],
        scratch_shapes=[pltpu.VMEM((tokens, slots, hidden), jnp.bfloat16)],
        name="back",
    )(d_two, slope, taps, kernel)
    d_input = d_input.reshape(tokens, CAP, sections, feat).transpose(2, 1, 0, 3)
    d_input = d_input.reshape(sections, CAP, width)
    extra = jnp.pad(gate_grad.reshape(CAP, sections).T[:, :, None], ((0, 0), (0, 0), (0, tail - 1)))
    back = exchange(jnp.concatenate([d_input, extra], axis=2))
    mine = jnp.dot(
        placing, back.reshape(slots, width + tail), preferred_element_type=jnp.float32
    ).astype(jnp.bfloat16)
    return (mine[:, :width].reshape(owned, side, side, feat), mine[:, width])


def solution(mesh):
    in_specs = (
        P("expert", None, None, "chan"),
        P("expert", None, None, "chan"),
        P("expert"),
        P("expert", None),
        P("expert", None, None, None, "chan"),
        P("expert", None, "chan"),
        P("expert", "chan", None),
    )
    out_specs = (P("expert", None, None, "chan"), P("expert"))
    return jax.shard_map(
        on_device, mesh=mesh, in_specs=in_specs, out_specs=out_specs, check_vma=False
    )
```

```python
import jax
import jax.numpy as jnp
from jax import lax
from jax.experimental import pallas as pl
from jax.experimental.pallas import tpu as pltpu
from jax.sharding import PartitionSpec as P

CAP = 2


def near(pos, off, side):
    row, col = pos // side + off // 3 - 1, pos % side + off % 3 - 1
    return row * side + col if 0 <= row < side and 0 <= col < side else None


def project_kernel(
    turn_ref, own_ref, next_ref, low_ref, high_ref, prev_ref, weight_ref, h_two_ref, gate_ref,
    d_two_ref, part_ref, left_ref, sums_ref,
):
    steps, rows, lanes = own_ref.shape
    half = lanes // 2
    tokens, slots, hidden = d_two_ref.shape
    own = slots // 2

    def block(kind, step):
        if kind == 2:
            ref, step = (low_ref, step) if step < steps // 2 else (high_ref, step - steps // 2)
        else:
            ref = (own_ref, next_ref, None, prev_ref)[kind]
        return ref[step]

    for turn in range(4):

        @pl.when(turn_ref[0] == turn)
        def _():
            for step in range(steps):
                for pair in range(2):
                    first = block((2 * pair - turn) % 4, step)
                    second = block((2 * pair + 1 - turn) % 4, step)
                    start = (2 * step + pair) * lanes
                    span = slice(start, start + lanes)
                    left_ref[:rows, span] = jnp.concatenate(
                        [first[:, :half], second[:, :half]], axis=1
                    )
                    left_ref[rows:, span] = jnp.concatenate(
                        [first[:, half:], second[:, half:]], axis=1
                    )

    wide = 256
    sums_ref[...] = jnp.zeros(sums_ref.shape, jnp.float32)
    for group in range(2):
        keep = slice(group * own, (group + 1) * own)
        scale = gate_ref[keep, :][:, :1]
        total = jnp.zeros((own, 128), jnp.float32)
        for start in range(0, hidden, wide):
            upper = lax.dot_general(
                left_ref[group * rows : (group + 1) * rows, :],
                weight_ref[start : start + wide, :],
                (((1,), (1,)), ((), ())),
                preferred_element_type=jnp.float32,
            )
            for pos in range(tokens):
                piece = upper[pos * own : (pos + 1) * own, :]
                d_two_ref[pos, keep, start : start + wide] = (piece * scale).astype(jnp.bfloat16)
                prod = h_two_ref[pos, keep, start : start + wide].astype(jnp.float32) * piece
                for lane in range(0, wide, 128):
                    total = total + prod[:, lane : lane + 128]
        sums_ref[keep, :] = total
    row = lax.dot_general(
        jnp.ones((8, 128), jnp.float32),
        sums_ref[...],
        (((1,), (1,)), ((), ())),
        preferred_element_type=jnp.float32,
        precision=lax.Precision.HIGHEST,
    )[:1]
    part_ref[...] = jnp.broadcast_to(row[None], part_ref.shape)


def back_kernel(d_two_ref, slope_ref, taps_ref, kernel_ref, d_in_ref, d_one_ref, *, side):
    tokens, slots, hidden = d_two_ref.shape
    wide = 256
    for start in range(0, hidden, wide):
        span = slice(start, start + wide)
        for pos in range(tokens):
            total = jnp.zeros((slots, wide), jnp.float32)
            for off in range(9):
                other = near(pos, 8 - off, side)
                if other is not None:
                    total = total + d_two_ref[other, :, span].astype(jnp.float32) * taps_ref[
                        off : off + 1, span
                    ].astype(jnp.float32)
            d_one_ref[pos, :, span] = (total * slope_ref[pos, :, span]).astype(jnp.bfloat16)
    for pos in range(tokens):
        total = jnp.zeros(d_in_ref.shape[1:], jnp.float32)
        for off in range(9):
            other = near(pos, 8 - off, side)
            if other is not None:
                total = total + lax.dot_general(
                    d_one_ref[other],
                    kernel_ref[off],
                    (((1,), (1,)), ((), ())),
                    preferred_element_type=jnp.float32,
                )
        d_in_ref[pos] = total.astype(jnp.bfloat16)


def vmem(count):
    return [pl.BlockSpec(memory_space=pltpu.VMEM) for _ in range(count)]


def forward(inputs, kernel, taps, side):
    tokens = side * side
    blank = jnp.zeros_like(inputs[0])
    columns = []
    for pos in range(tokens):
        picked = [near(pos, off, side) for off in range(9)]
        columns.append(
            jnp.concatenate([blank if n is None else inputs[n] for n in picked], axis=1)
        )
    h_one = jnp.einsum(
        "psk,kf->psf",
        jnp.stack(columns),
        kernel.reshape(-1, kernel.shape[2]),
        preferred_element_type=jnp.float32,
    )
    active = jax.nn.gelu(h_one, approximate=False).astype(jnp.bfloat16)
    grid = active.reshape(side, side, *active.shape[1:])
    padded = jnp.pad(grid, ((1, 1), (1, 1), (0, 0), (0, 0))).astype(jnp.float32)
    total = jnp.zeros(grid.shape, jnp.float32)
    for row in range(3):
        for col in range(3):
            total = total + padded[row : row + side, col : col + side] * taps[3 * row + col].astype(
                jnp.float32
            )
    h_two = total.reshape(active.shape).astype(jnp.bfloat16)
    cdf = 0.5 * (1.0 + lax.erf(h_one * 0.7071067811865476))
    slope = cdf + h_one * jnp.exp(-0.5 * h_one * h_one) * 0.3989422804014327
    return h_two, slope


def on_device(tiles_in, grad_out, gate, expert_id, w_conv, w_depth, w_out):
    owned, side, _, feat = tiles_in.shape
    tokens = side * side
    width = tokens * feat
    sections = lax.axis_size("expert")
    slots = sections * CAP
    hidden = w_out.shape[1]
    group = w_conv.shape[3]
    chosen = expert_id[:, 0]
    matches = (chosen[:, None] == jnp.arange(sections, dtype=jnp.int32)[None, :]).astype(jnp.int32)
    rows = jnp.arange(owned, dtype=jnp.int32)
    earlier = (rows[:, None] > rows[None, :]) & (chosen[:, None] == chosen[None, :])
    rank = jnp.sum(earlier.astype(jnp.int32), axis=1)
    slot = chosen * CAP + rank
    placing = (slot[:, None] == jnp.arange(slots, dtype=jnp.int32)[None, :]).astype(jnp.bfloat16)

    def place(array):
        out = lax.dot_general(
            placing, array, (((0,), (0,)), ((), ())), preferred_element_type=jnp.float32
        )
        return out.astype(jnp.bfloat16).reshape(sections, CAP, -1)

    def exchange(array):
        return lax.all_to_all(array, "expert", split_axis=0, concat_axis=0, tiled=True)

    tail = 64
    both = 2 * width
    extra = jnp.pad(gate[:, None], ((0, 0), (0, tail - 1)))
    flat = jnp.concatenate(
        [grad_out.reshape(owned, width), tiles_in.reshape(owned, width), extra], axis=1
    )
    arrived = exchange(place(flat))
    packed = arrived[:, :, :width].reshape(sections, CAP, tokens, feat).transpose(2, 0, 1, 3)
    packed = packed.reshape(tokens * sections, CAP * feat)
    chans = lax.axis_size("chan")
    steps = chans // 4
    families = [[4 * step + kind for step in range(steps)] for kind in range(4)]
    own = lax.all_gather(packed, "chan", axis=0, axis_index_groups=families)

    def shift(array, by):
        return lax.ppermute(array, "chan", [(c, (c + by) % chans) for c in range(chans)])

    low = shift(own[: steps // 2], 2)
    high = shift(own[steps // 2 :], -2)
    prev = shift(own, 1)
    following = shift(own, -1)
    turn = (lax.axis_index("chan") % 4).astype(jnp.int32).reshape(1)

    inputs = arrived[:, :, width:both].reshape(sections, CAP, tokens, feat).transpose(2, 1, 0, 3)
    inputs = inputs.reshape(tokens, slots, feat)
    gates = arrived[:, :, both].T.reshape(slots, 1).astype(jnp.float32)
    gates = jnp.broadcast_to(gates, (slots, 128))
    taps = w_depth[0]
    small = w_conv[0].reshape(9, group, hidden)
    count = feat // group
    per = hidden // count
    which = jnp.arange(hidden, dtype=jnp.int32) // per
    kernel = jnp.concatenate(
        [jnp.where(which == g, small, jnp.zeros_like(small)) for g in range(count)], axis=1
    )
    h_two, slope = forward(inputs, kernel, taps, side)

    d_two, part = pl.pallas_call(
        project_kernel,
        out_shape=(
            jax.ShapeDtypeStruct((tokens, slots, hidden), jnp.bfloat16),
            jax.ShapeDtypeStruct((chans, 1, 128), jnp.float32),
        ),
        in_specs=[pl.BlockSpec(memory_space=pltpu.SMEM)] + vmem(8),
        out_specs=tuple(vmem(2)),
        scratch_shapes=[
            pltpu.VMEM((tokens * slots, w_out.shape[2]), jnp.bfloat16),
            pltpu.VMEM((128, 128), jnp.float32),
        ],
        name="project",
    )(turn, own, following, low, high, prev, w_out[0], h_two, gates)
    parts = lax.all_to_all(part, "chan", split_axis=0, concat_axis=0, tiled=True)
    gate_grad = jnp.sum(parts[:, 0], axis=0)[:slots].astype(jnp.bfloat16)
    d_input = pl.pallas_call(
        lambda *refs: back_kernel(*refs, side=side),
        out_shape=jax.ShapeDtypeStruct((tokens, slots, feat), jnp.bfloat16),
        in_specs=vmem(4),
        out_specs=vmem(1)[0],
        scratch_shapes=[pltpu.VMEM((tokens, slots, hidden), jnp.bfloat16)],
        name="back",
    )(d_two, slope, taps, kernel)
    d_input = d_input.reshape(tokens, CAP, sections, feat).transpose(2, 1, 0, 3)
    d_input = d_input.reshape(sections, CAP, width)
    extra = jnp.pad(gate_grad.reshape(CAP, sections).T[:, :, None], ((0, 0), (0, 0), (0, tail - 1)))
    back = exchange(jnp.concatenate([d_input, extra], axis=2))
    mine = jnp.dot(
        placing, back.reshape(slots, width + tail), preferred_element_type=jnp.float32
    ).astype(jnp.bfloat16)
    return (mine[:, :width].reshape(owned, side, side, feat), mine[:, width])


def solution(mesh):
    in_specs = (
        P("expert", None, None, "chan"),
        P("expert", None, None, "chan"),
        P("expert"),
        P("expert", None),
        P("expert", None, None, None, "chan"),
        P("expert", None, "chan"),
        P("expert", "chan", None),
    )
    out_specs = (P("expert", None, None, "chan"), P("expert"))
    return jax.shard_map(
        on_device, mesh=mesh, in_specs=in_specs, out_specs=out_specs, check_vma=False
    )
```

```python
import jax
import jax.numpy as jnp
from jax import lax
from jax.experimental import pallas as pl
from jax.experimental.pallas import tpu as pltpu
from jax.sharding import PartitionSpec as P

CAP = 2


def near(pos, off, side):
    row, col = pos // side + off // 3 - 1, pos % side + off % 3 - 1
    return row * side + col if 0 <= row < side and 0 <= col < side else None


def prep_kernel(ids_ref, gate_ref, grads_ref, tiles_ref, out_ref):
    tokens, owned, feat = grads_ref.shape
    sections = out_ref.shape[0]
    ids = ids_ref[...]
    rows = lax.broadcasted_iota(jnp.int32, (owned, owned), 0)
    cols = lax.broadcasted_iota(jnp.int32, (owned, owned), 1)
    wide = jnp.broadcast_to(ids, (owned, owned))
    column = jnp.sum(jnp.where(rows == cols, wide, 0), axis=1, keepdims=True)
    earlier = jnp.where((rows < cols) & (column == wide), 1, 0)
    rank = jnp.sum(earlier, axis=0, keepdims=True)
    named = jnp.broadcast_to(ids, (sections, owned)) == lax.broadcasted_iota(
        jnp.int32, (sections, owned), 0
    )
    turn = jnp.broadcast_to(rank, (sections, owned))
    picks = [jnp.where(named & (turn == r), 1.0, 0.0).astype(jnp.bfloat16) for r in range(CAP)]
    gates = jnp.broadcast_to(gate_ref[...].astype(jnp.float32), (owned, owned))
    gates = jnp.sum(jnp.where(rows == cols, gates, 0.0), axis=1, keepdims=True)
    gates = jnp.broadcast_to(gates, (owned, feat)).astype(jnp.bfloat16)
    fields = [grads_ref[pos] for pos in range(tokens)]
    fields += [tiles_ref[pos] for pos in range(tokens)] + [gates]
    lines = []
    for field in fields:
        halves = [jnp.dot(pick, field, preferred_element_type=jnp.float32) for pick in picks]
        lines.append(jnp.concatenate(halves, axis=1))
    while len(lines) < out_ref.shape[1]:
        lines.append(jnp.zeros_like(lines[0]))
    out_ref[...] = jnp.swapaxes(jnp.stack(lines), 0, 1).astype(jnp.bfloat16)


def sort_kernel(in_ref, packed_ref, inputs_ref, gates_ref):
    tokens, slots, feat = inputs_ref.shape
    own = slots // 2
    lines = jnp.swapaxes(in_ref[...].astype(jnp.float32), 0, 1)
    for pos in range(tokens):
        packed_ref[pos * own : (pos + 1) * own, :] = lines[pos].astype(jnp.bfloat16)
        field = lines[tokens + pos]
        inputs_ref[pos] = jnp.concatenate([field[:, :feat], field[:, feat:]], axis=0).astype(
            jnp.bfloat16
        )
    field = lines[2 * tokens]
    for group in range(2):
        part = field[:, group * feat : (group + 1) * feat]
        gates_ref[group * own : (group + 1) * own, :] = jnp.concatenate([part, part], axis=1)


def forward_kernel(
    inputs_ref, kernel_ref, taps_ref, h_two_ref, slope_ref, act_ref, *, side
):
    tokens, slots, hidden = h_two_ref.shape
    wide = 256
    for start in range(0, hidden, wide):
        span = slice(start, start + wide)
        for pos in range(tokens):
            value = jnp.zeros((slots, wide), jnp.float32)
            for off in range(9):
                other = near(pos, off, side)
                if other is not None:
                    value = value + jnp.dot(
                        inputs_ref[other],
                        kernel_ref[off, :, span],
                        preferred_element_type=jnp.float32,
                    )
            cdf = 0.5 * (1.0 + lax.erf(value * 0.7071067811865476))
            act_ref[pos, :, span] = (value * cdf).astype(jnp.bfloat16).astype(jnp.float32)
            slope_ref[pos, :, span] = (
                cdf + value * jnp.exp(-0.5 * value * value) * 0.3989422804014327
            )
        taps = [taps_ref[off : off + 1, span].astype(jnp.float32) for off in range(9)]
        for pos in range(tokens):
            total = jnp.zeros((slots, wide), jnp.float32)
            for off in range(9):
                other = near(pos, off, side)
                if other is not None:
                    total = total + act_ref[other, :, span] * taps[off]
            h_two_ref[pos, :, span] = total.astype(jnp.bfloat16)


def project_kernel(
    turn_ref, own_ref, next_ref, low_ref, high_ref, prev_ref, weight_ref, h_two_ref, gate_ref,
    d_two_ref, part_ref, left_ref, sums_ref,
):
    steps, rows, lanes = own_ref.shape
    half = lanes // 2
    tokens, slots, hidden = d_two_ref.shape
    own = slots // 2

    def block(kind, step):
        if kind == 2:
            ref, step = (low_ref, step) if step < steps // 2 else (high_ref, step - steps // 2)
        else:
            ref = (own_ref, next_ref, None, prev_ref)[kind]
        return ref[step]

    for turn in range(4):

        @pl.when(turn_ref[0] == turn)
        def _():
            for step in range(steps):
                for pair in range(2):
                    first = block((2 * pair - turn) % 4, step)
                    second = block((2 * pair + 1 - turn) % 4, step)
                    start = (2 * step + pair) * lanes
                    span = slice(start, start + lanes)
                    left_ref[:rows, span] = jnp.concatenate(
                        [first[:, :half], second[:, :half]], axis=1
                    )
                    left_ref[rows:, span] = jnp.concatenate(
                        [first[:, half:], second[:, half:]], axis=1
                    )

    wide = 256
    sums_ref[...] = jnp.zeros(sums_ref.shape, jnp.float32)
    for group in range(2):
        keep = slice(group * own, (group + 1) * own)
        scale = gate_ref[keep, :][:, :1]
        total = jnp.zeros((own, 128), jnp.float32)
        for start in range(0, hidden, wide):
            upper = lax.dot_general(
                left_ref[group * rows : (group + 1) * rows, :],
                weight_ref[start : start + wide, :],
                (((1,), (1,)), ((), ())),
                preferred_element_type=jnp.float32,
            )
            for pos in range(tokens):
                piece = upper[pos * own : (pos + 1) * own, :]
                d_two_ref[pos, keep, start : start + wide] = (piece * scale).astype(jnp.bfloat16)
                prod = h_two_ref[pos, keep, start : start + wide].astype(jnp.float32) * piece
                for lane in range(0, wide, 128):
                    total = total + prod[:, lane : lane + 128]
        sums_ref[keep, :] = total
    row = lax.dot_general(
        jnp.ones((8, 128), jnp.float32),
        sums_ref[...],
        (((1,), (1,)), ((), ())),
        preferred_element_type=jnp.float32,
        precision=lax.Precision.HIGHEST,
    )[:1]
    part_ref[...] = jnp.broadcast_to(row[None], part_ref.shape)


def back_kernel(d_two_ref, slope_ref, taps_ref, kernel_ref, d_in_ref, d_one_ref, *, side):
    tokens, slots, hidden = d_two_ref.shape
    wide = 256
    for start in range(0, hidden, wide):
        span = slice(start, start + wide)
        for pos in range(tokens):
            total = jnp.zeros((slots, wide), jnp.float32)
            for off in range(9):
                other = near(pos, 8 - off, side)
                if other is not None:
                    total = total + d_two_ref[other, :, span].astype(jnp.float32) * taps_ref[
                        off : off + 1, span
                    ].astype(jnp.float32)
            d_one_ref[pos, :, span] = (total * slope_ref[pos, :, span]).astype(jnp.bfloat16)
    for pos in range(tokens):
        total = jnp.zeros(d_in_ref.shape[1:], jnp.float32)
        for off in range(9):
            other = near(pos, 8 - off, side)
            if other is not None:
                total = total + lax.dot_general(
                    d_one_ref[other],
                    kernel_ref[off],
                    (((1,), (1,)), ((), ())),
                    preferred_element_type=jnp.float32,
                )
        d_in_ref[pos] = total.astype(jnp.bfloat16)


def vmem(count):
    return [pl.BlockSpec(memory_space=pltpu.VMEM) for _ in range(count)]


def on_device(tiles_in, grad_out, gate, expert_id, w_conv, w_depth, w_out):
    owned, side, _, feat = tiles_in.shape
    tokens = side * side
    width = tokens * feat
    sections = lax.axis_size("expert")
    slots = sections * CAP
    hidden = w_out.shape[1]
    group = w_conv.shape[3]
    chosen = expert_id[:, 0]
    matches = (chosen[:, None] == jnp.arange(sections, dtype=jnp.int32)[None, :]).astype(jnp.int32)
    rows = jnp.arange(owned, dtype=jnp.int32)
    earlier = (rows[:, None] > rows[None, :]) & (chosen[:, None] == chosen[None, :])
    rank = jnp.sum(earlier.astype(jnp.int32), axis=1)
    slot = chosen * CAP + rank
    placing = (slot[:, None] == jnp.arange(slots, dtype=jnp.int32)[None, :]).astype(jnp.bfloat16)

    def exchange(array):
        return lax.all_to_all(array, "expert", split_axis=0, concat_axis=0, tiled=True)

    tail = 64
    lines = -(-(2 * tokens + 1) // 8) * 8
    outward = pl.pallas_call(
        prep_kernel,
        out_shape=jax.ShapeDtypeStruct((sections, lines, CAP * feat), jnp.bfloat16),
        in_specs=vmem(4),
        out_specs=vmem(1)[0],
        name="prep",
    )(
        expert_id.reshape(1, owned),
        gate.reshape(1, owned),
        grad_out.transpose(1, 2, 0, 3).reshape(tokens, owned, feat),
        tiles_in.transpose(1, 2, 0, 3).reshape(tokens, owned, feat),
    )
    arrived = exchange(outward)
    packed, inputs, gates = pl.pallas_call(
        sort_kernel,
        out_shape=(
            jax.ShapeDtypeStruct((tokens * sections, CAP * feat), jnp.bfloat16),
            jax.ShapeDtypeStruct((tokens, slots, feat), jnp.bfloat16),
            jax.ShapeDtypeStruct((slots, 128), jnp.float32),
        ),
        in_specs=vmem(1),
        out_specs=tuple(vmem(3)),
        name="sort",
    )(arrived)
    chans = lax.axis_size("chan")
    steps = chans // 4
    families = [[4 * step + kind for step in range(steps)] for kind in range(4)]
    own = lax.all_gather(packed, "chan", axis=0, axis_index_groups=families)

    def shift(array, by):
        return lax.ppermute(array, "chan", [(c, (c + by) % chans) for c in range(chans)])

    low = shift(own[: steps // 2], 2)
    high = shift(own[steps // 2 :], -2)
    prev = shift(own, 1)
    following = shift(own, -1)
    turn = (lax.axis_index("chan") % 4).astype(jnp.int32).reshape(1)

    taps = w_depth[0]
    small = w_conv[0].reshape(9, group, hidden)
    count = feat // group
    per = hidden // count
    which = jnp.arange(hidden, dtype=jnp.int32) // per
    kernel = jnp.concatenate(
        [jnp.where(which == g, small, jnp.zeros_like(small)) for g in range(count)], axis=1
    )
    h_two, slope = pl.pallas_call(
        lambda *refs: forward_kernel(*refs, side=side),
        out_shape=(
            jax.ShapeDtypeStruct((tokens, slots, hidden), jnp.bfloat16),
            jax.ShapeDtypeStruct((tokens, slots, hidden), jnp.float32),
        ),
        in_specs=vmem(3),
        out_specs=tuple(vmem(2)),
        scratch_shapes=[pltpu.VMEM((tokens, slots, hidden), jnp.float32)],
        name="forward",
    )(inputs, kernel, taps)

    d_two, part = pl.pallas_call(
        project_kernel,
        out_shape=(
            jax.ShapeDtypeStruct((tokens, slots, hidden), jnp.bfloat16),
            jax.ShapeDtypeStruct((chans, 1, 128), jnp.float32),
        ),
        in_specs=[pl.BlockSpec(memory_space=pltpu.SMEM)] + vmem(8),
        out_specs=tuple(vmem(2)),
        scratch_shapes=[
            pltpu.VMEM((tokens * slots, w_out.shape[2]), jnp.bfloat16),
            pltpu.VMEM((128, 128), jnp.float32),
        ],
        name="project",
    )(turn, own, following, low, high, prev, w_out[0], h_two, gates)
    parts = lax.all_to_all(part, "chan", split_axis=0, concat_axis=0, tiled=True)
    gate_grad = jnp.sum(parts[:, 0], axis=0)[:slots].astype(jnp.bfloat16)
    d_input = pl.pallas_call(
        lambda *refs: back_kernel(*refs, side=side),
        out_shape=jax.ShapeDtypeStruct((tokens, slots, feat), jnp.bfloat16),
        in_specs=vmem(4),
        out_specs=vmem(1)[0],
        scratch_shapes=[pltpu.VMEM((tokens, slots, hidden), jnp.bfloat16)],
        name="back",
    )(d_two, slope, taps, kernel)
    d_input = d_input.reshape(tokens, CAP, sections, feat).transpose(2, 1, 0, 3)
    d_input = d_input.reshape(sections, CAP, width)
    extra = jnp.pad(gate_grad.reshape(CAP, sections).T[:, :, None], ((0, 0), (0, 0), (0, tail - 1)))
    back = exchange(jnp.concatenate([d_input, extra], axis=2))
    mine = jnp.dot(
        placing, back.reshape(slots, width + tail), preferred_element_type=jnp.float32
    ).astype(jnp.bfloat16)
    return (mine[:, :width].reshape(owned, side, side, feat), mine[:, width])


def solution(mesh):
    in_specs = (
        P("expert", None, None, "chan"),
        P("expert", None, None, "chan"),
        P("expert"),
        P("expert", None),
        P("expert", None, None, None, "chan"),
        P("expert", None, "chan"),
        P("expert", "chan", None),
    )
    out_specs = (P("expert", None, None, "chan"), P("expert"))
    return jax.shard_map(
        on_device, mesh=mesh, in_specs=in_specs, out_specs=out_specs, check_vma=False
    )
```

```python
import jax
import jax.numpy as jnp
from jax import lax
from jax.experimental import pallas as pl
from jax.experimental.pallas import tpu as pltpu
from jax.sharding import PartitionSpec as P

CAP = 2


def near(pos, off, side):
    row, col = pos // side + off // 3 - 1, pos % side + off % 3 - 1
    return row * side + col if 0 <= row < side and 0 <= col < side else None


def prep_kernel(ids_ref, gate_ref, grads_ref, tiles_ref, out_ref):
    tokens, owned, feat = grads_ref.shape
    sections = out_ref.shape[0]
    ids = ids_ref[...]
    rows = lax.broadcasted_iota(jnp.int32, (owned, owned), 0)
    cols = lax.broadcasted_iota(jnp.int32, (owned, owned), 1)
    wide = jnp.broadcast_to(ids, (owned, owned))
    column = jnp.sum(jnp.where(rows == cols, wide, 0), axis=1, keepdims=True)
    earlier = jnp.where((rows < cols) & (column == wide), 1, 0)
    rank = jnp.sum(earlier, axis=0, keepdims=True)
    named = jnp.broadcast_to(ids, (sections, owned)) == lax.broadcasted_iota(
        jnp.int32, (sections, owned), 0
    )
    turn = jnp.broadcast_to(rank, (sections, owned))
    picks = [jnp.where(named & (turn == r), 1.0, 0.0).astype(jnp.bfloat16) for r in range(CAP)]
    gates = jnp.broadcast_to(gate_ref[...].astype(jnp.float32), (owned, owned))
    gates = jnp.sum(jnp.where(rows == cols, gates, 0.0), axis=1, keepdims=True)
    gates = jnp.broadcast_to(gates, (owned, feat)).astype(jnp.bfloat16)
    fields = [grads_ref[pos] for pos in range(tokens)]
    fields += [tiles_ref[pos] for pos in range(tokens)] + [gates]
    lines = []
    for field in fields:
        halves = [jnp.dot(pick, field, preferred_element_type=jnp.float32) for pick in picks]
        lines.append(jnp.concatenate(halves, axis=1))
    while len(lines) < out_ref.shape[1]:
        lines.append(jnp.zeros_like(lines[0]))
    out_ref[...] = jnp.swapaxes(jnp.stack(lines), 0, 1).astype(jnp.bfloat16)


def sort_kernel(in_ref, packed_ref, inputs_ref, gates_ref):
    tokens, slots, feat = inputs_ref.shape
    own = slots // 2
    lines = jnp.swapaxes(in_ref[...].astype(jnp.float32), 0, 1)
    for pos in range(tokens):
        packed_ref[pos * own : (pos + 1) * own, :] = lines[pos].astype(jnp.bfloat16)
        field = lines[tokens + pos]
        inputs_ref[pos] = jnp.concatenate([field[:, :feat], field[:, feat:]], axis=0).astype(
            jnp.bfloat16
        )
    field = lines[2 * tokens]
    for group in range(2):
        part = field[:, group * feat : (group + 1) * feat]
        gates_ref[group * own : (group + 1) * own, :] = jnp.concatenate([part, part], axis=1)


def forward_kernel(
    inputs_ref, kernel_ref, taps_ref, h_two_ref, slope_ref, act_ref, *, side
):
    tokens, slots, hidden = h_two_ref.shape
    wide = 256
    for start in range(0, hidden, wide):
        span = slice(start, start + wide)
        for pos in range(tokens):
            value = jnp.zeros((slots, wide), jnp.float32)
            for off in range(9):
                other = near(pos, off, side)
                if other is not None:
                    value = value + jnp.dot(
                        inputs_ref[other],
                        kernel_ref[off, :, span],
                        preferred_element_type=jnp.float32,
                    )
            cdf = 0.5 * (1.0 + lax.erf(value * 0.7071067811865476))
            act_ref[pos, :, span] = (value * cdf).astype(jnp.bfloat16).astype(jnp.float32)
            slope_ref[pos, :, span] = (
                cdf + value * jnp.exp(-0.5 * value * value) * 0.3989422804014327
            )
        taps = [taps_ref[off : off + 1, span].astype(jnp.float32) for off in range(9)]
        for pos in range(tokens):
            total = jnp.zeros((slots, wide), jnp.float32)
            for off in range(9):
                other = near(pos, off, side)
                if other is not None:
                    total = total + act_ref[other, :, span] * taps[off]
            h_two_ref[pos, :, span] = total.astype(jnp.bfloat16)


def early_kernel(turn_ref, own_ref, next_ref, prev_ref, weight_ref, upper_ref, late_ref, left_ref):
    steps, rows, lanes = own_ref.shape
    half = lanes // 2
    hidden = weight_ref.shape[0]
    blank = jnp.zeros((rows, half), jnp.bfloat16)

    for turn in range(4):

        @pl.when(turn_ref[0] == turn)
        def _():
            for step in range(steps):
                for pair in range(2):
                    kinds = [(2 * pair + side - turn) % 4 for side in range(2)]
                    refs = [(own_ref, next_ref, None, prev_ref)[kind] for kind in kinds]
                    blocks = [None if ref is None else ref[step] for ref in refs]
                    start = (2 * step + pair) * lanes
                    for group in range(2):
                        part = slice(group * half, (group + 1) * half)
                        left_ref[group * rows : (group + 1) * rows, start : start + lanes] = (
                            jnp.concatenate(
                                [blank if x is None else x[:, part] for x in blocks], axis=1
                            )
                        )
            for step in range(0, steps, 2):
                cuts = []
                for inner in range(2):
                    start = (4 * (step + inner) + (turn + 2) % 4) * half
                    cuts.append(weight_ref[:, start : start + half])
                late_ref[:, step * half : (step + 2) * half] = jnp.concatenate(cuts, axis=1)

    wide = 256
    for start in range(0, hidden, wide):
        upper_ref[:, start : start + wide] = lax.dot_general(
            left_ref[...],
            weight_ref[start : start + wide, :],
            (((1,), (1,)), ((), ())),
            preferred_element_type=jnp.float32,
        )


def project_kernel(
    low_ref, high_ref, late_ref, upper_ref, h_two_ref, gate_ref, d_two_ref, part_ref,
    left_ref, sums_ref,
):
    steps, rows, lanes = low_ref.shape
    half = lanes // 2
    tokens, slots, wide = d_two_ref.shape
    own = slots // 2

    @pl.when(pl.program_id(0) == 0)
    def _():
        sums_ref[...] = jnp.zeros(sums_ref.shape, jnp.float32)
        for place, ref in enumerate((low_ref, high_ref)):
            for step in range(0, steps, 2):
                start = (place * steps + step) * half
                for group in range(2):
                    part = slice(group * half, (group + 1) * half)
                    left_ref[group * rows : (group + 1) * rows, start : start + lanes] = (
                        jnp.concatenate([ref[step][:, part], ref[step + 1][:, part]], axis=1)
                    )

    rest = lax.dot_general(
        left_ref[...], late_ref[...], (((1,), (1,)), ((), ())), preferred_element_type=jnp.float32
    )
    for group in range(2):
        keep = slice(group * own, (group + 1) * own)
        scale = gate_ref[keep, :][:, :1]
        total = sums_ref[keep, :]
        for pos in range(tokens):
            row = group * rows + pos * own
            piece = upper_ref[row : row + own, :] + rest[row : row + own, :]
            d_two_ref[pos, keep, :] = (piece * scale).astype(jnp.bfloat16)
            prod = h_two_ref[pos, keep, :].astype(jnp.float32) * piece
            for lane in range(0, wide, 128):
                total = total + prod[:, lane : lane + 128]
        sums_ref[keep, :] = total

    @pl.when(pl.program_id(0) == pl.num_programs(0) - 1)
    def _():
        row = lax.dot_general(
            jnp.ones((8, 128), jnp.float32),
            sums_ref[...],
            (((1,), (1,)), ((), ())),
            preferred_element_type=jnp.float32,
            precision=lax.Precision.HIGHEST,
        )[:1]
        part_ref[...] = jnp.broadcast_to(row[None], part_ref.shape)


def back_kernel(d_two_ref, slope_ref, taps_ref, kernel_ref, d_in_ref, d_one_ref, *, side):
    tokens, slots, hidden = d_two_ref.shape
    wide = 256
    for start in range(0, hidden, wide):
        span = slice(start, start + wide)
        for pos in range(tokens):
            total = jnp.zeros((slots, wide), jnp.float32)
            for off in range(9):
                other = near(pos, 8 - off, side)
                if other is not None:
                    total = total + d_two_ref[other, :, span].astype(jnp.float32) * taps_ref[
                        off : off + 1, span
                    ].astype(jnp.float32)
            d_one_ref[pos, :, span] = (total * slope_ref[pos, :, span]).astype(jnp.bfloat16)
    for pos in range(tokens):
        total = jnp.zeros(d_in_ref.shape[1:], jnp.float32)
        for off in range(9):
            other = near(pos, 8 - off, side)
            if other is not None:
                total = total + lax.dot_general(
                    d_one_ref[other],
                    kernel_ref[off],
                    (((1,), (1,)), ((), ())),
                    preferred_element_type=jnp.float32,
                )
        d_in_ref[pos] = total.astype(jnp.bfloat16)


def vmem(count):
    return [pl.BlockSpec(memory_space=pltpu.VMEM) for _ in range(count)]


def on_device(tiles_in, grad_out, gate, expert_id, w_conv, w_depth, w_out):
    owned, side, _, feat = tiles_in.shape
    tokens = side * side
    width = tokens * feat
    sections = lax.axis_size("expert")
    slots = sections * CAP
    hidden = w_out.shape[1]
    group = w_conv.shape[3]
    chosen = expert_id[:, 0]
    matches = (chosen[:, None] == jnp.arange(sections, dtype=jnp.int32)[None, :]).astype(jnp.int32)
    rows = jnp.arange(owned, dtype=jnp.int32)
    earlier = (rows[:, None] > rows[None, :]) & (chosen[:, None] == chosen[None, :])
    rank = jnp.sum(earlier.astype(jnp.int32), axis=1)
    slot = chosen * CAP + rank
    placing = (slot[:, None] == jnp.arange(slots, dtype=jnp.int32)[None, :]).astype(jnp.bfloat16)

    def exchange(array):
        return lax.all_to_all(array, "expert", split_axis=0, concat_axis=0, tiled=True)

    tail = 64
    lines = -(-(2 * tokens + 1) // 8) * 8
    outward = pl.pallas_call(
        prep_kernel,
        out_shape=jax.ShapeDtypeStruct((sections, lines, CAP * feat), jnp.bfloat16),
        in_specs=vmem(4),
        out_specs=vmem(1)[0],
        name="prep",
    )(
        expert_id.reshape(1, owned),
        gate.reshape(1, owned),
        grad_out.transpose(1, 2, 0, 3).reshape(tokens, owned, feat),
        tiles_in.transpose(1, 2, 0, 3).reshape(tokens, owned, feat),
    )
    arrived = exchange(outward)
    packed, inputs, gates = pl.pallas_call(
        sort_kernel,
        out_shape=(
            jax.ShapeDtypeStruct((tokens * sections, CAP * feat), jnp.bfloat16),
            jax.ShapeDtypeStruct((tokens, slots, feat), jnp.bfloat16),
            jax.ShapeDtypeStruct((slots, 128), jnp.float32),
        ),
        in_specs=vmem(1),
        out_specs=tuple(vmem(3)),
        name="sort",
    )(arrived)
    chans = lax.axis_size("chan")
    steps = chans // 4
    families = [[4 * step + kind for step in range(steps)] for kind in range(4)]
    own = lax.all_gather(packed, "chan", axis=0, axis_index_groups=families)

    def shift(array, by):
        return lax.ppermute(array, "chan", [(c, (c + by) % chans) for c in range(chans)])

    low = shift(own[: steps // 2], 2)
    high = shift(own[steps // 2 :], -2)
    prev = shift(own, 1)
    following = shift(own, -1)
    turn = (lax.axis_index("chan") % 4).astype(jnp.int32).reshape(1)

    taps = w_depth[0]
    small = w_conv[0].reshape(9, group, hidden)
    count = feat // group
    per = hidden // count
    which = jnp.arange(hidden, dtype=jnp.int32) // per
    kernel = jnp.concatenate(
        [jnp.where(which == g, small, jnp.zeros_like(small)) for g in range(count)], axis=1
    )
    h_two, slope = pl.pallas_call(
        lambda *refs: forward_kernel(*refs, side=side),
        out_shape=(
            jax.ShapeDtypeStruct((tokens, slots, hidden), jnp.bfloat16),
            jax.ShapeDtypeStruct((tokens, slots, hidden), jnp.float32),
        ),
        in_specs=vmem(3),
        out_specs=tuple(vmem(2)),
        scratch_shapes=[pltpu.VMEM((tokens, slots, hidden), jnp.float32)],
        name="forward",
    )(inputs, kernel, taps)

    features = w_out.shape[2]
    upper, late = pl.pallas_call(
        early_kernel,
        out_shape=(
            jax.ShapeDtypeStruct((tokens * slots, hidden), jnp.float32),
            jax.ShapeDtypeStruct((hidden, features // 4), jnp.bfloat16),
        ),
        in_specs=[pl.BlockSpec(memory_space=pltpu.SMEM)] + vmem(4),
        out_specs=tuple(vmem(2)),
        scratch_shapes=[pltpu.VMEM((tokens * slots, features), jnp.bfloat16)],
        name="early",
    )(turn, own, following, prev, w_out[0])
    wide = 256
    whole = lambda shape: pl.BlockSpec(shape, lambda i: (0,) * len(shape))
    d_two, part = pl.pallas_call(
        project_kernel,
        grid=(hidden // wide,),
        out_shape=(
            jax.ShapeDtypeStruct((tokens, slots, hidden), jnp.bfloat16),
            jax.ShapeDtypeStruct((chans, 1, 128), jnp.float32),
        ),
        in_specs=[
            whole(low.shape),
            whole(high.shape),
            pl.BlockSpec((wide, features // 4), lambda i: (i, 0)),
            pl.BlockSpec((tokens * slots, wide), lambda i: (0, i)),
            pl.BlockSpec((tokens, slots, wide), lambda i: (0, 0, i)),
            whole(gates.shape),
        ],
        out_specs=(
            pl.BlockSpec((tokens, slots, wide), lambda i: (0, 0, i)),
            whole((chans, 1, 128)),
        ),
        scratch_shapes=[
            pltpu.VMEM((tokens * slots, features // 4), jnp.bfloat16),
            pltpu.VMEM((128, 128), jnp.float32),
        ],
        name="project",
    )(low, high, late, upper, h_two, gates)
    parts = lax.all_to_all(part, "chan", split_axis=0, concat_axis=0, tiled=True)
    gate_grad = jnp.sum(parts[:, 0], axis=0)[:slots].astype(jnp.bfloat16)
    d_input = pl.pallas_call(
        lambda *refs: back_kernel(*refs, side=side),
        out_shape=jax.ShapeDtypeStruct((tokens, slots, feat), jnp.bfloat16),
        in_specs=vmem(4),
        out_specs=vmem(1)[0],
        scratch_shapes=[pltpu.VMEM((tokens, slots, hidden), jnp.bfloat16)],
        name="back",
    )(d_two, slope, taps, kernel)
    d_input = d_input.reshape(tokens, CAP, sections, feat).transpose(2, 1, 0, 3)
    d_input = d_input.reshape(sections, CAP, width)
    extra = jnp.pad(gate_grad.reshape(CAP, sections).T[:, :, None], ((0, 0), (0, 0), (0, tail - 1)))
    back = exchange(jnp.concatenate([d_input, extra], axis=2))
    mine = jnp.dot(
        placing, back.reshape(slots, width + tail), preferred_element_type=jnp.float32
    ).astype(jnp.bfloat16)
    return (mine[:, :width].reshape(owned, side, side, feat), mine[:, width])


def solution(mesh):
    in_specs = (
        P("expert", None, None, "chan"),
        P("expert", None, None, "chan"),
        P("expert"),
        P("expert", None),
        P("expert", None, None, None, "chan"),
        P("expert", None, "chan"),
        P("expert", "chan", None),
    )
    out_specs = (P("expert", None, None, "chan"), P("expert"))
    return jax.shard_map(
        on_device, mesh=mesh, in_specs=in_specs, out_specs=out_specs, check_vma=False
    )
```

```python
import jax
import jax.numpy as jnp
from jax import lax
from jax.experimental import pallas as pl
from jax.experimental.pallas import tpu as pltpu
from jax.sharding import PartitionSpec as P


CAP = 2


def near(pos, off, side):
    row, col = pos // side + off // 3 - 1, pos % side + off % 3 - 1
    return row * side + col if 0 <= row < side and 0 <= col < side else None


def prep_kernel(ids_ref, gate_ref, grads_ref, tiles_ref, out_ref):
    tokens, owned, feat = grads_ref.shape
    sections = out_ref.shape[0]
    ids = ids_ref[...]
    rows = lax.broadcasted_iota(jnp.int32, (owned, owned), 0)
    cols = lax.broadcasted_iota(jnp.int32, (owned, owned), 1)
    wide = jnp.broadcast_to(ids, (owned, owned))
    column = jnp.sum(jnp.where(rows == cols, wide, 0), axis=1, keepdims=True)
    earlier = jnp.where((rows < cols) & (column == wide), 1, 0)
    rank = jnp.sum(earlier, axis=0, keepdims=True)
    named = jnp.broadcast_to(ids, (sections, owned)) == lax.broadcasted_iota(
        jnp.int32, (sections, owned), 0
    )
    turn = jnp.broadcast_to(rank, (sections, owned))
    picks = [jnp.where(named & (turn == r), 1.0, 0.0).astype(jnp.bfloat16) for r in range(CAP)]
    gates = jnp.broadcast_to(gate_ref[...].astype(jnp.float32), (owned, owned))
    gates = jnp.sum(jnp.where(rows == cols, gates, 0.0), axis=1, keepdims=True)
    gates = jnp.broadcast_to(gates, (owned, feat)).astype(jnp.bfloat16)
    fields = [grads_ref[pos] for pos in range(tokens)]
    fields += [tiles_ref[pos] for pos in range(tokens)] + [gates]
    lines = []
    for field in fields:
        halves = [jnp.dot(pick, field, preferred_element_type=jnp.float32) for pick in picks]
        lines.append(jnp.concatenate(halves, axis=1))
    while len(lines) < out_ref.shape[1]:
        lines.append(jnp.zeros_like(lines[0]))
    out_ref[...] = jnp.swapaxes(jnp.stack(lines), 0, 1).astype(jnp.bfloat16)


def sort_kernel(in_ref, packed_ref, inputs_ref, gates_ref):
    tokens, slots, feat = inputs_ref.shape
    own = slots // 2
    lines = jnp.swapaxes(in_ref[...].astype(jnp.float32), 0, 1)
    for pos in range(tokens):
        packed_ref[pos * own : (pos + 1) * own, :] = lines[pos].astype(jnp.bfloat16)
        field = lines[tokens + pos]
        inputs_ref[pos] = jnp.concatenate([field[:, :feat], field[:, feat:]], axis=0).astype(
            jnp.bfloat16
        )
    field = lines[2 * tokens]
    for group in range(2):
        part = field[:, group * feat : (group + 1) * feat]
        gates_ref[group * own : (group + 1) * own, :] = jnp.concatenate([part, part], axis=1)


def forward_kernel(
    inputs_ref, kernel_ref, taps_ref, h_two_ref, slope_ref, act_ref, *, side
):
    tokens, slots, hidden = h_two_ref.shape
    wide = 256
    for start in range(0, hidden, wide):
        span = slice(start, start + wide)
        for pos in range(tokens):
            value = jnp.zeros((slots, wide), jnp.float32)
            for off in range(9):
                other = near(pos, off, side)
                if other is not None:
                    value = value + jnp.dot(
                        inputs_ref[other],
                        kernel_ref[off, :, span],
                        preferred_element_type=jnp.float32,
                    )
            cdf = 0.5 * (1.0 + lax.erf(value * 0.7071067811865476))
            act_ref[pos, :, span] = (value * cdf).astype(jnp.bfloat16).astype(jnp.float32)
            slope_ref[pos, :, span] = (
                cdf + value * jnp.exp(-0.5 * value * value) * 0.3989422804014327
            )
        taps = [taps_ref[off : off + 1, span].astype(jnp.float32) for off in range(9)]
        for pos in range(tokens):
            total = jnp.zeros((slots, wide), jnp.float32)
            for off in range(9):
                other = near(pos, off, side)
                if other is not None:
                    total = total + act_ref[other, :, span] * taps[off]
            h_two_ref[pos, :, span] = total.astype(jnp.bfloat16)


def early_kernel(turn_ref, own_ref, next_ref, prev_ref, weight_ref, upper_ref, late_ref, left_ref):
    steps, rows, lanes = own_ref.shape
    half = lanes // 2
    hidden = weight_ref.shape[0]
    blank = jnp.zeros((rows, half), jnp.bfloat16)

    for turn in range(4):

        @pl.when(turn_ref[0] == turn)
        def _():
            for step in range(steps):
                for pair in range(2):
                    kinds = [(2 * pair + side - turn) % 4 for side in range(2)]
                    refs = [(own_ref, next_ref, None, prev_ref)[kind] for kind in kinds]
                    blocks = [None if ref is None else ref[step] for ref in refs]
                    start = (2 * step + pair) * lanes
                    for group in range(2):
                        part = slice(group * half, (group + 1) * half)
                        left_ref[group * rows : (group + 1) * rows, start : start + lanes] = (
                            jnp.concatenate(
                                [blank if x is None else x[:, part] for x in blocks], axis=1
                            )
                        )
            for step in range(0, steps, 2):
                cuts = []
                for inner in range(2):
                    start = (4 * (step + inner) + (turn + 2) % 4) * half
                    cuts.append(weight_ref[:, start : start + half])
                late_ref[:, step * half : (step + 2) * half] = jnp.concatenate(cuts, axis=1)

    wide = 256
    for start in range(0, hidden, wide):
        upper_ref[:, start : start + wide] = lax.dot_general(
            left_ref[...],
            weight_ref[start : start + wide, :],
            (((1,), (1,)), ((), ())),
            preferred_element_type=jnp.float32,
        )


def project_kernel(
    low_ref, high_ref, late_ref, upper_ref, h_two_ref, gate_ref, d_two_ref, part_ref,
    left_ref, sums_ref,
):
    steps, rows, lanes = low_ref.shape
    half = lanes // 2
    tokens, slots, wide = d_two_ref.shape
    own = slots // 2

    @pl.when(pl.program_id(0) == 0)
    def _():
        sums_ref[...] = jnp.zeros(sums_ref.shape, jnp.float32)
        for place, ref in enumerate((low_ref, high_ref)):
            for step in range(0, steps, 2):
                start = (place * steps + step) * half
                for group in range(2):
                    part = slice(group * half, (group + 1) * half)
                    left_ref[group * rows : (group + 1) * rows, start : start + lanes] = (
                        jnp.concatenate([ref[step][:, part], ref[step + 1][:, part]], axis=1)
                    )

    rest = lax.dot_general(
        left_ref[...], late_ref[...], (((1,), (1,)), ((), ())), preferred_element_type=jnp.float32
    )
    for group in range(2):
        keep = slice(group * own, (group + 1) * own)
        scale = gate_ref[keep, :][:, :1]
        total = sums_ref[keep, :]
        for pos in range(tokens):
            row = group * rows + pos * own
            piece = upper_ref[row : row + own, :] + rest[row : row + own, :]
            d_two_ref[pos, keep, :] = (piece * scale).astype(jnp.bfloat16)
            prod = h_two_ref[pos, keep, :].astype(jnp.float32) * piece
            for lane in range(0, wide, 128):
                total = total + prod[:, lane : lane + 128]
        sums_ref[keep, :] = total

    @pl.when(pl.program_id(0) == pl.num_programs(0) - 1)
    def _():
        row = lax.dot_general(
            jnp.ones((8, 128), jnp.float32),
            sums_ref[...],
            (((1,), (1,)), ((), ())),
            preferred_element_type=jnp.float32,
            precision=lax.Precision.HIGHEST,
        )[:1]
        part_ref[...] = jnp.broadcast_to(row[None], part_ref.shape)


def back_kernel(d_two_ref, slope_ref, taps_ref, kernel_ref, d_in_ref, d_one_ref, *, side):
    tokens, slots, hidden = d_two_ref.shape
    wide = 256
    for start in range(0, hidden, wide):
        span = slice(start, start + wide)
        for pos in range(tokens):
            total = jnp.zeros((slots, wide), jnp.float32)
            for off in range(9):
                other = near(pos, 8 - off, side)
                if other is not None:
                    total = total + d_two_ref[other, :, span].astype(jnp.float32) * taps_ref[
                        off : off + 1, span
                    ].astype(jnp.float32)
            d_one_ref[pos, :, span] = (total * slope_ref[pos, :, span]).astype(jnp.bfloat16)
    for pos in range(tokens):
        total = jnp.zeros(d_in_ref.shape[1:], jnp.float32)
        for off in range(9):
            other = near(pos, 8 - off, side)
            if other is not None:
                total = total + lax.dot_general(
                    d_one_ref[other],
                    kernel_ref[off],
                    (((1,), (1,)), ((), ())),
                    preferred_element_type=jnp.float32,
                )
        d_in_ref[pos] = total.astype(jnp.bfloat16)


def near_by(array):
    return pltpu.with_memory_space_constraint(array, pltpu.VMEM)


def vmem(count):
    return [pl.BlockSpec(memory_space=pltpu.VMEM) for _ in range(count)]


def on_device(tiles_in, grad_out, gate, expert_id, w_conv, w_depth, w_out):
    owned, side, _, feat = tiles_in.shape
    tokens = side * side
    width = tokens * feat
    sections = lax.axis_size("expert")
    slots = sections * CAP
    hidden = w_out.shape[1]
    group = w_conv.shape[3]
    chosen = expert_id[:, 0]
    matches = (chosen[:, None] == jnp.arange(sections, dtype=jnp.int32)[None, :]).astype(jnp.int32)
    rows = jnp.arange(owned, dtype=jnp.int32)
    earlier = (rows[:, None] > rows[None, :]) & (chosen[:, None] == chosen[None, :])
    rank = jnp.sum(earlier.astype(jnp.int32), axis=1)
    slot = chosen * CAP + rank
    placing = (slot[:, None] == jnp.arange(slots, dtype=jnp.int32)[None, :]).astype(jnp.bfloat16)

    def exchange(array):
        return lax.all_to_all(array, "expert", split_axis=0, concat_axis=0, tiled=True)

    tail = 64
    lines = -(-(2 * tokens + 1) // 8) * 8
    outward = pl.pallas_call(
        prep_kernel,
        out_shape=jax.ShapeDtypeStruct((sections, lines, CAP * feat), jnp.bfloat16),
        in_specs=vmem(4),
        out_specs=vmem(1)[0],
        compiler_params=pltpu.CompilerParams(vmem_limit_bytes=24 << 20),
        name="prep",
    )(
        expert_id.reshape(1, owned),
        gate.reshape(1, owned),
        grad_out.transpose(1, 2, 0, 3).reshape(tokens, owned, feat),
        tiles_in.transpose(1, 2, 0, 3).reshape(tokens, owned, feat),
    )
    arrived = exchange(outward)
    packed, inputs, gates = pl.pallas_call(
        sort_kernel,
        out_shape=(
            jax.ShapeDtypeStruct((tokens * sections, CAP * feat), jnp.bfloat16),
            jax.ShapeDtypeStruct((tokens, slots, feat), jnp.bfloat16),
            jax.ShapeDtypeStruct((slots, 128), jnp.float32),
        ),
        in_specs=vmem(1),
        out_specs=tuple(vmem(3)),
        compiler_params=pltpu.CompilerParams(vmem_limit_bytes=24 << 20),
        name="sort",
    )(near_by(arrived))
    chans = lax.axis_size("chan")
    steps = chans // 4
    families = [[4 * step + kind for step in range(steps)] for kind in range(4)]
    own = lax.all_gather(packed, "chan", axis=0, axis_index_groups=families)

    def shift(array, by):
        return lax.ppermute(array, "chan", [(c, (c + by) % chans) for c in range(chans)])

    prev = shift(own, 1)
    following = shift(own, -1)
    low = shift(prev[: steps // 2], 1)
    high = shift(following[steps // 2 :], -1)
    turn = (lax.axis_index("chan") % 4).astype(jnp.int32).reshape(1)

    taps = w_depth[0]
    small = w_conv[0].reshape(9, group, hidden)
    count = feat // group
    per = hidden // count
    which = jnp.arange(hidden, dtype=jnp.int32) // per
    kernel = jnp.concatenate(
        [jnp.where(which == g, small, jnp.zeros_like(small)) for g in range(count)], axis=1
    )
    h_two, slope = pl.pallas_call(
        lambda *refs: forward_kernel(*refs, side=side),
        out_shape=(
            jax.ShapeDtypeStruct((tokens, slots, hidden), jnp.bfloat16),
            jax.ShapeDtypeStruct((tokens, slots, hidden), jnp.float32),
        ),
        in_specs=vmem(3),
        out_specs=tuple(vmem(2)),
        scratch_shapes=[pltpu.VMEM((tokens, slots, hidden), jnp.float32)],
        compiler_params=pltpu.CompilerParams(vmem_limit_bytes=24 << 20),
        name="forward",
    )(inputs, kernel, taps)

    features = w_out.shape[2]
    upper, late = pl.pallas_call(
        early_kernel,
        out_shape=(
            jax.ShapeDtypeStruct((tokens * slots, hidden), jnp.float32),
            jax.ShapeDtypeStruct((hidden, features // 4), jnp.bfloat16),
        ),
        in_specs=[pl.BlockSpec(memory_space=pltpu.SMEM)] + vmem(4),
        out_specs=tuple(vmem(2)),
        scratch_shapes=[pltpu.VMEM((tokens * slots, features), jnp.bfloat16)],
        compiler_params=pltpu.CompilerParams(vmem_limit_bytes=24 << 20),
        name="early",
    )(turn, near_by(own), near_by(following), near_by(prev), near_by(w_out[0]))
    wide = 256
    whole = lambda shape: pl.BlockSpec(shape, lambda i: (0,) * len(shape))
    d_two, part = pl.pallas_call(
        project_kernel,
        grid=(hidden // wide,),
        out_shape=(
            jax.ShapeDtypeStruct((tokens, slots, hidden), jnp.bfloat16),
            jax.ShapeDtypeStruct((chans, 1, 128), jnp.float32),
        ),
        in_specs=[
            whole(low.shape),
            whole(high.shape),
            pl.BlockSpec((wide, features // 4), lambda i: (i, 0)),
            pl.BlockSpec((tokens * slots, wide), lambda i: (0, i)),
            pl.BlockSpec((tokens, slots, wide), lambda i: (0, 0, i)),
            whole(gates.shape),
        ],
        out_specs=(
            pl.BlockSpec((tokens, slots, wide), lambda i: (0, 0, i)),
            whole((chans, 1, 128)),
        ),
        scratch_shapes=[
            pltpu.VMEM((tokens * slots, features // 4), jnp.bfloat16),
            pltpu.VMEM((128, 128), jnp.float32),
        ],
        compiler_params=pltpu.CompilerParams(vmem_limit_bytes=24 << 20),
        name="project",
    )(near_by(low), near_by(high), late, upper, h_two, gates)
    parts = lax.all_to_all(part, "chan", split_axis=0, concat_axis=0, tiled=True)
    gate_grad = jnp.sum(parts[:, 0], axis=0)[:slots].astype(jnp.bfloat16)
    d_input = pl.pallas_call(
        lambda *refs: back_kernel(*refs, side=side),
        out_shape=jax.ShapeDtypeStruct((tokens, slots, feat), jnp.bfloat16),
        in_specs=vmem(4),
        out_specs=vmem(1)[0],
        scratch_shapes=[pltpu.VMEM((tokens, slots, hidden), jnp.bfloat16)],
        compiler_params=pltpu.CompilerParams(vmem_limit_bytes=24 << 20),
        name="back",
    )(d_two, slope, taps, kernel)
    d_input = d_input.reshape(tokens, CAP, sections, feat).transpose(2, 1, 0, 3)
    d_input = d_input.reshape(sections, CAP, width)
    extra = jnp.pad(gate_grad.reshape(CAP, sections).T[:, :, None], ((0, 0), (0, 0), (0, tail - 1)))
    back = exchange(jnp.concatenate([d_input, extra], axis=2))
    mine = jnp.dot(
        placing, back.reshape(slots, width + tail), preferred_element_type=jnp.float32
    ).astype(jnp.bfloat16)
    return (mine[:, :width].reshape(owned, side, side, feat), mine[:, width])


def solution(mesh):
    in_specs = (
        P("expert", None, None, "chan"),
        P("expert", None, None, "chan"),
        P("expert"),
        P("expert", None),
        P("expert", None, None, None, "chan"),
        P("expert", None, "chan"),
        P("expert", "chan", None),
    )
    out_specs = (P("expert", None, None, "chan"), P("expert"))
    return jax.shard_map(
        on_device, mesh=mesh, in_specs=in_specs, out_specs=out_specs, check_vma=False
    )
```

```python
import jax
import jax.numpy as jnp
from jax import lax
from jax.experimental import pallas as pl
from jax.experimental.pallas import tpu as pltpu
from jax.sharding import PartitionSpec as P


CAP = 2


def near(pos, off, side):
    row, col = pos // side + off // 3 - 1, pos % side + off % 3 - 1
    return row * side + col if 0 <= row < side and 0 <= col < side else None


def prep_kernel(ids_ref, gate_ref, grads_ref, tiles_ref, out_ref):
    tokens, owned, feat = grads_ref.shape
    sections = out_ref.shape[0]
    ids = ids_ref[...]
    rows = lax.broadcasted_iota(jnp.int32, (owned, owned), 0)
    cols = lax.broadcasted_iota(jnp.int32, (owned, owned), 1)
    wide = jnp.broadcast_to(ids, (owned, owned))
    column = jnp.sum(jnp.where(rows == cols, wide, 0), axis=1, keepdims=True)
    earlier = jnp.where((rows < cols) & (column == wide), 1, 0)
    rank = jnp.sum(earlier, axis=0, keepdims=True)
    named = jnp.broadcast_to(ids, (sections, owned)) == lax.broadcasted_iota(
        jnp.int32, (sections, owned), 0
    )
    turn = jnp.broadcast_to(rank, (sections, owned))
    picks = [jnp.where(named & (turn == r), 1.0, 0.0).astype(jnp.bfloat16) for r in range(CAP)]
    gates = jnp.broadcast_to(gate_ref[...].astype(jnp.float32), (owned, owned))
    gates = jnp.sum(jnp.where(rows == cols, gates, 0.0), axis=1, keepdims=True)
    gates = jnp.broadcast_to(gates, (owned, feat)).astype(jnp.bfloat16)
    fields = [grads_ref[pos] for pos in range(tokens)]
    fields += [tiles_ref[pos] for pos in range(tokens)] + [gates]
    lines = []
    for field in fields:
        halves = [jnp.dot(pick, field, preferred_element_type=jnp.float32) for pick in picks]
        lines.append(jnp.concatenate(halves, axis=1))
    while len(lines) < out_ref.shape[1]:
        lines.append(jnp.zeros_like(lines[0]))
    out_ref[...] = jnp.swapaxes(jnp.stack(lines), 0, 1).astype(jnp.bfloat16)


def sort_kernel(in_ref, packed_ref, inputs_ref, gates_ref):
    tokens, slots, feat = inputs_ref.shape
    own = slots // 2
    lines = jnp.swapaxes(in_ref[...].astype(jnp.float32), 0, 1)
    for pos in range(tokens):
        packed_ref[pos * own : (pos + 1) * own, :] = lines[pos].astype(jnp.bfloat16)
        field = lines[tokens + pos]
        inputs_ref[pos] = jnp.concatenate([field[:, :feat], field[:, feat:]], axis=0).astype(
            jnp.bfloat16
        )
    field = lines[2 * tokens]
    for group in range(2):
        part = field[:, group * feat : (group + 1) * feat]
        gates_ref[group * own : (group + 1) * own, :] = jnp.concatenate([part, part], axis=1)


def forward_kernel(
    inputs_ref, kernel_ref, taps_ref, h_two_ref, slope_ref, act_ref, *, side
):
    tokens, slots, hidden = h_two_ref.shape
    wide = 256
    for start in range(0, hidden, wide):
        span = slice(start, start + wide)
        for pos in range(tokens):
            value = jnp.zeros((slots, wide), jnp.float32)
            for off in range(9):
                other = near(pos, off, side)
                if other is not None:
                    value = value + jnp.dot(
                        inputs_ref[other],
                        kernel_ref[off, :, span],
                        preferred_element_type=jnp.float32,
                    )
            cdf = 0.5 * (1.0 + lax.erf(value * 0.7071067811865476))
            act_ref[pos, :, span] = (value * cdf).astype(jnp.bfloat16).astype(jnp.float32)
            slope_ref[pos, :, span] = (
                cdf + value * jnp.exp(-0.5 * value * value) * 0.3989422804014327
            )
        taps = [taps_ref[off : off + 1, span].astype(jnp.float32) for off in range(9)]
        for pos in range(tokens):
            total = jnp.zeros((slots, wide), jnp.float32)
            for off in range(9):
                other = near(pos, off, side)
                if other is not None:
                    total = total + act_ref[other, :, span] * taps[off]
            h_two_ref[pos, :, span] = total.astype(jnp.bfloat16)


def split_kernel(in_ref, low_ref, high_ref):
    steps = low_ref.shape[0]
    low_ref[...] = in_ref[:steps]
    high_ref[...] = in_ref[steps:]


def early_kernel(
    turn_ref, own_low, own_high, next_low, next_high, prev_low, prev_high, weight_ref,
    upper_ref, late_ref, left_ref,
):
    part_steps, rows, lanes = own_low.shape
    steps = 2 * part_steps
    families = ((own_low, own_high), (next_low, next_high), None, (prev_low, prev_high))
    half = lanes // 2
    hidden = weight_ref.shape[0]
    blank = jnp.zeros((rows, half), jnp.bfloat16)

    for turn in range(4):

        @pl.when(turn_ref[0] == turn)
        def _():
            for step in range(steps):
                for pair in range(2):
                    kinds = [(2 * pair + side - turn) % 4 for side in range(2)]
                    refs = [families[kind] for kind in kinds]
                    blocks = [
                        None if ref is None else ref[step // part_steps][step % part_steps]
                        for ref in refs
                    ]
                    start = (2 * step + pair) * lanes
                    for group in range(2):
                        part = slice(group * half, (group + 1) * half)
                        left_ref[group * rows : (group + 1) * rows, start : start + lanes] = (
                            jnp.concatenate(
                                [blank if x is None else x[:, part] for x in blocks], axis=1
                            )
                        )
            for step in range(0, steps, 2):
                cuts = []
                for inner in range(2):
                    start = (4 * (step + inner) + (turn + 2) % 4) * half
                    cuts.append(weight_ref[:, start : start + half])
                late_ref[:, step * half : (step + 2) * half] = jnp.concatenate(cuts, axis=1)

    wide = 256
    for start in range(0, hidden, wide):
        upper_ref[:, start : start + wide] = lax.dot_general(
            left_ref[...],
            weight_ref[start : start + wide, :],
            (((1,), (1,)), ((), ())),
            preferred_element_type=jnp.float32,
        )


def project_kernel(
    low_ref, high_ref, late_ref, upper_ref, h_two_ref, gate_ref, d_two_ref, part_ref,
    left_ref, sums_ref,
):
    steps, rows, lanes = low_ref.shape
    half = lanes // 2
    tokens, slots, wide = d_two_ref.shape
    own = slots // 2

    @pl.when(pl.program_id(0) == 0)
    def _():
        sums_ref[...] = jnp.zeros(sums_ref.shape, jnp.float32)
        for place, ref in enumerate((low_ref, high_ref)):
            for step in range(0, steps, 2):
                start = (place * steps + step) * half
                for group in range(2):
                    part = slice(group * half, (group + 1) * half)
                    left_ref[group * rows : (group + 1) * rows, start : start + lanes] = (
                        jnp.concatenate([ref[step][:, part], ref[step + 1][:, part]], axis=1)
                    )

    rest = lax.dot_general(
        left_ref[...], late_ref[...], (((1,), (1,)), ((), ())), preferred_element_type=jnp.float32
    )
    for group in range(2):
        keep = slice(group * own, (group + 1) * own)
        scale = gate_ref[keep, :][:, :1]
        total = sums_ref[keep, :]
        for pos in range(tokens):
            row = group * rows + pos * own
            piece = upper_ref[row : row + own, :] + rest[row : row + own, :]
            d_two_ref[pos, keep, :] = (piece * scale).astype(jnp.bfloat16)
            prod = h_two_ref[pos, keep, :].astype(jnp.float32) * piece
            for lane in range(0, wide, 128):
                total = total + prod[:, lane : lane + 128]
        sums_ref[keep, :] = total

    @pl.when(pl.program_id(0) == pl.num_programs(0) - 1)
    def _():
        row = lax.dot_general(
            jnp.ones((8, 128), jnp.float32),
            sums_ref[...],
            (((1,), (1,)), ((), ())),
            preferred_element_type=jnp.float32,
            precision=lax.Precision.HIGHEST,
        )[:1]
        part_ref[...] = jnp.broadcast_to(row[None], part_ref.shape)


def back_kernel(d_two_ref, slope_ref, taps_ref, kernel_ref, d_in_ref, d_one_ref, *, side):
    tokens, slots, hidden = d_two_ref.shape
    wide = 256
    for start in range(0, hidden, wide):
        span = slice(start, start + wide)
        for pos in range(tokens):
            total = jnp.zeros((slots, wide), jnp.float32)
            for off in range(9):
                other = near(pos, 8 - off, side)
                if other is not None:
                    total = total + d_two_ref[other, :, span].astype(jnp.float32) * taps_ref[
                        off : off + 1, span
                    ].astype(jnp.float32)
            d_one_ref[pos, :, span] = (total * slope_ref[pos, :, span]).astype(jnp.bfloat16)
    for pos in range(tokens):
        total = jnp.zeros(d_in_ref.shape[1:], jnp.float32)
        for off in range(9):
            other = near(pos, 8 - off, side)
            if other is not None:
                total = total + lax.dot_general(
                    d_one_ref[other],
                    kernel_ref[off],
                    (((1,), (1,)), ((), ())),
                    preferred_element_type=jnp.float32,
                )
        d_in_ref[pos] = total.astype(jnp.bfloat16)


def near_by(array):
    return pltpu.with_memory_space_constraint(array, pltpu.VMEM)


def vmem(count):
    return [pl.BlockSpec(memory_space=pltpu.VMEM) for _ in range(count)]


def on_device(tiles_in, grad_out, gate, expert_id, w_conv, w_depth, w_out):
    owned, side, _, feat = tiles_in.shape
    tokens = side * side
    width = tokens * feat
    sections = lax.axis_size("expert")
    slots = sections * CAP
    hidden = w_out.shape[1]
    group = w_conv.shape[3]
    chosen = expert_id[:, 0]
    matches = (chosen[:, None] == jnp.arange(sections, dtype=jnp.int32)[None, :]).astype(jnp.int32)
    rows = jnp.arange(owned, dtype=jnp.int32)
    earlier = (rows[:, None] > rows[None, :]) & (chosen[:, None] == chosen[None, :])
    rank = jnp.sum(earlier.astype(jnp.int32), axis=1)
    slot = chosen * CAP + rank
    placing = (slot[:, None] == jnp.arange(slots, dtype=jnp.int32)[None, :]).astype(jnp.bfloat16)

    def exchange(array):
        return lax.all_to_all(array, "expert", split_axis=0, concat_axis=0, tiled=True)

    tail = 64
    lines = -(-(2 * tokens + 1) // 8) * 8
    outward = pl.pallas_call(
        prep_kernel,
        out_shape=jax.ShapeDtypeStruct((sections, lines, CAP * feat), jnp.bfloat16),
        in_specs=vmem(4),
        out_specs=vmem(1)[0],
        name="prep",
    )(
        expert_id.reshape(1, owned),
        gate.reshape(1, owned),
        grad_out.transpose(1, 2, 0, 3).reshape(tokens, owned, feat),
        tiles_in.transpose(1, 2, 0, 3).reshape(tokens, owned, feat),
    )
    arrived = exchange(outward)
    packed, inputs, gates = pl.pallas_call(
        sort_kernel,
        out_shape=(
            jax.ShapeDtypeStruct((tokens * sections, CAP * feat), jnp.bfloat16),
            jax.ShapeDtypeStruct((tokens, slots, feat), jnp.bfloat16),
            jax.ShapeDtypeStruct((slots, 128), jnp.float32),
        ),
        in_specs=vmem(1),
        out_specs=tuple(vmem(3)),
        compiler_params=pltpu.CompilerParams(vmem_limit_bytes=24 << 20),
        name="sort",
    )(near_by(arrived))
    chans = lax.axis_size("chan")
    steps = chans // 4
    families = [[4 * step + kind for step in range(steps)] for kind in range(4)]
    own = lax.all_gather(packed, "chan", axis=0, axis_index_groups=families)

    def shift(array, by):
        return lax.ppermute(array, "chan", [(c, (c + by) % chans) for c in range(chans)])

    part = jax.ShapeDtypeStruct((steps // 2, *own.shape[1:]), own.dtype)
    own_low, own_high = pl.pallas_call(
        split_kernel,
        out_shape=(part, part),
        in_specs=vmem(1),
        out_specs=tuple(vmem(2)),
        compiler_params=pltpu.CompilerParams(vmem_limit_bytes=24 << 20),
        name="split",
    )(near_by(own))
    prev_low = shift(own_low, 1)
    next_high = shift(own_high, -1)
    prev_high = shift(own_high, 1)
    next_low = shift(own_low, -1)
    low = shift(prev_low, 1)
    high = shift(next_high, -1)
    turn = (lax.axis_index("chan") % 4).astype(jnp.int32).reshape(1)

    taps = w_depth[0]
    small = w_conv[0].reshape(9, group, hidden)
    count = feat // group
    per = hidden // count
    which = jnp.arange(hidden, dtype=jnp.int32) // per
    kernel = jnp.concatenate(
        [jnp.where(which == g, small, jnp.zeros_like(small)) for g in range(count)], axis=1
    )
    h_two, slope = pl.pallas_call(
        lambda *refs: forward_kernel(*refs, side=side),
        out_shape=(
            jax.ShapeDtypeStruct((tokens, slots, hidden), jnp.bfloat16),
            jax.ShapeDtypeStruct((tokens, slots, hidden), jnp.float32),
        ),
        in_specs=vmem(3),
        out_specs=tuple(vmem(2)),
        scratch_shapes=[pltpu.VMEM((tokens, slots, hidden), jnp.float32)],
        compiler_params=pltpu.CompilerParams(vmem_limit_bytes=24 << 20),
        name="forward",
    )(inputs, kernel, taps)

    features = w_out.shape[2]
    upper, late = pl.pallas_call(
        early_kernel,
        out_shape=(
            jax.ShapeDtypeStruct((tokens * slots, hidden), jnp.float32),
            jax.ShapeDtypeStruct((hidden, features // 4), jnp.bfloat16),
        ),
        in_specs=[pl.BlockSpec(memory_space=pltpu.SMEM)] + vmem(7),
        out_specs=tuple(vmem(2)),
        scratch_shapes=[pltpu.VMEM((tokens * slots, features), jnp.bfloat16)],
        compiler_params=pltpu.CompilerParams(vmem_limit_bytes=24 << 20),
        name="early",
    )(
        turn,
        *[near_by(x) for x in (own_low, own_high, next_low, next_high, prev_low, prev_high)],
        near_by(w_out[0]),
    )
    wide = 256
    whole = lambda shape: pl.BlockSpec(shape, lambda i: (0,) * len(shape))
    d_two, part = pl.pallas_call(
        project_kernel,
        grid=(hidden // wide,),
        out_shape=(
            jax.ShapeDtypeStruct((tokens, slots, hidden), jnp.bfloat16),
            jax.ShapeDtypeStruct((chans, 1, 128), jnp.float32),
        ),
        in_specs=[
            whole(low.shape),
            whole(high.shape),
            pl.BlockSpec((wide, features // 4), lambda i: (i, 0)),
            pl.BlockSpec((tokens * slots, wide), lambda i: (0, i)),
            pl.BlockSpec((tokens, slots, wide), lambda i: (0, 0, i)),
            whole(gates.shape),
        ],
        out_specs=(
            pl.BlockSpec((tokens, slots, wide), lambda i: (0, 0, i)),
            whole((chans, 1, 128)),
        ),
        scratch_shapes=[
            pltpu.VMEM((tokens * slots, features // 4), jnp.bfloat16),
            pltpu.VMEM((128, 128), jnp.float32),
        ],
        compiler_params=pltpu.CompilerParams(vmem_limit_bytes=24 << 20),
        name="project",
    )(near_by(low), near_by(high), late, upper, h_two, gates)
    parts = lax.all_to_all(part, "chan", split_axis=0, concat_axis=0, tiled=True)
    gate_grad = jnp.sum(parts[:, 0], axis=0)[:slots].astype(jnp.bfloat16)
    d_input = pl.pallas_call(
        lambda *refs: back_kernel(*refs, side=side),
        out_shape=jax.ShapeDtypeStruct((tokens, slots, feat), jnp.bfloat16),
        in_specs=vmem(4),
        out_specs=vmem(1)[0],
        scratch_shapes=[pltpu.VMEM((tokens, slots, hidden), jnp.bfloat16)],
        compiler_params=pltpu.CompilerParams(vmem_limit_bytes=24 << 20),
        name="back",
    )(d_two, slope, taps, kernel)
    d_input = d_input.reshape(tokens, CAP, sections, feat).transpose(2, 1, 0, 3)
    d_input = d_input.reshape(sections, CAP, width)
    extra = jnp.pad(gate_grad.reshape(CAP, sections).T[:, :, None], ((0, 0), (0, 0), (0, tail - 1)))
    back = exchange(jnp.concatenate([d_input, extra], axis=2))
    mine = jnp.dot(
        placing, back.reshape(slots, width + tail), preferred_element_type=jnp.float32
    ).astype(jnp.bfloat16)
    return (mine[:, :width].reshape(owned, side, side, feat), mine[:, width])


def solution(mesh):
    in_specs = (
        P("expert", None, None, "chan"),
        P("expert", None, None, "chan"),
        P("expert"),
        P("expert", None),
        P("expert", None, None, None, "chan"),
        P("expert", None, "chan"),
        P("expert", "chan", None),
    )
    out_specs = (P("expert", None, None, "chan"), P("expert"))
    return jax.shard_map(
        on_device, mesh=mesh, in_specs=in_specs, out_specs=out_specs, check_vma=False
    )
```

```python
import jax
import jax.numpy as jnp
from jax import lax
from jax.experimental import pallas as pl
from jax.experimental.pallas import tpu as pltpu
from jax.sharding import PartitionSpec as P


CAP = 2


def near(pos, off, side):
    row, col = pos // side + off // 3 - 1, pos % side + off % 3 - 1
    return row * side + col if 0 <= row < side and 0 <= col < side else None


def prep_kernel(ids_ref, gate_ref, grads_ref, tiles_ref, out_ref):
    tokens, owned, feat = grads_ref.shape
    sections = out_ref.shape[0]
    ids = ids_ref[...]
    rows = lax.broadcasted_iota(jnp.int32, (owned, owned), 0)
    cols = lax.broadcasted_iota(jnp.int32, (owned, owned), 1)
    wide = jnp.broadcast_to(ids, (owned, owned))
    column = jnp.sum(jnp.where(rows == cols, wide, 0), axis=1, keepdims=True)
    earlier = jnp.where((rows < cols) & (column == wide), 1, 0)
    rank = jnp.sum(earlier, axis=0, keepdims=True)
    named = jnp.broadcast_to(ids, (sections, owned)) == lax.broadcasted_iota(
        jnp.int32, (sections, owned), 0
    )
    turn = jnp.broadcast_to(rank, (sections, owned))
    picks = [jnp.where(named & (turn == r), 1.0, 0.0).astype(jnp.bfloat16) for r in range(CAP)]
    gates = jnp.broadcast_to(gate_ref[...].astype(jnp.float32), (owned, owned))
    gates = jnp.sum(jnp.where(rows == cols, gates, 0.0), axis=1, keepdims=True)
    gates = jnp.broadcast_to(gates, (owned, feat)).astype(jnp.bfloat16)
    fields = [grads_ref[pos] for pos in range(tokens)]
    fields += [tiles_ref[pos] for pos in range(tokens)] + [gates]
    lines = []
    for field in fields:
        halves = [jnp.dot(pick, field, preferred_element_type=jnp.float32) for pick in picks]
        lines.append(jnp.concatenate(halves, axis=1))
    while len(lines) < out_ref.shape[1]:
        lines.append(jnp.zeros_like(lines[0]))
    out_ref[...] = jnp.swapaxes(jnp.stack(lines), 0, 1).astype(jnp.bfloat16)


def sort_kernel(in_ref, packed_ref, inputs_ref, gates_ref):
    tokens, slots, feat = inputs_ref.shape
    own = slots // 2
    lines = jnp.swapaxes(in_ref[...].astype(jnp.float32), 0, 1)
    for pos in range(tokens):
        packed_ref[pos * own : (pos + 1) * own, :] = lines[pos].astype(jnp.bfloat16)
        field = lines[tokens + pos]
        inputs_ref[pos] = jnp.concatenate([field[:, :feat], field[:, feat:]], axis=0).astype(
            jnp.bfloat16
        )
    field = lines[2 * tokens]
    for group in range(2):
        part = field[:, group * feat : (group + 1) * feat]
        gates_ref[group * own : (group + 1) * own, :] = jnp.concatenate([part, part], axis=1)


def forward_kernel(
    inputs_ref, kernel_ref, taps_ref, h_two_ref, slope_ref, act_ref, *, side
):
    tokens, slots, hidden = h_two_ref.shape
    wide = 256
    for start in range(0, hidden, wide):
        span = slice(start, start + wide)
        for pos in range(tokens):
            value = jnp.zeros((slots, wide), jnp.float32)
            for off in range(9):
                other = near(pos, off, side)
                if other is not None:
                    value = value + jnp.dot(
                        inputs_ref[other],
                        kernel_ref[off, :, span],
                        preferred_element_type=jnp.float32,
                    )
            cdf = 0.5 * (1.0 + lax.erf(value * 0.7071067811865476))
            act_ref[pos, :, span] = (value * cdf).astype(jnp.bfloat16).astype(jnp.float32)
            slope_ref[pos, :, span] = (
                cdf + value * jnp.exp(-0.5 * value * value) * 0.3989422804014327
            )
        taps = [taps_ref[off : off + 1, span].astype(jnp.float32) for off in range(9)]
        for pos in range(tokens):
            total = jnp.zeros((slots, wide), jnp.float32)
            for off in range(9):
                other = near(pos, off, side)
                if other is not None:
                    total = total + act_ref[other, :, span] * taps[off]
            h_two_ref[pos, :, span] = total.astype(jnp.bfloat16)


def split_kernel(in_ref, low_ref, high_ref):
    steps = low_ref.shape[0]
    low_ref[...] = in_ref[:steps]
    high_ref[...] = in_ref[steps:]


def early_kernel(
    turn_ref, own_low, own_high, next_low, next_high, prev_low, prev_high, weight_ref,
    upper_ref, late_ref, left_ref,
):
    part_steps, rows, lanes = own_low.shape
    steps = 2 * part_steps
    families = ((own_low, own_high), (next_low, next_high), None, (prev_low, prev_high))
    half = lanes // 2
    hidden = weight_ref.shape[0]
    blank = jnp.zeros((rows, half), jnp.bfloat16)

    for turn in range(4):

        @pl.when(turn_ref[0] == turn)
        def _():
            for step in range(steps):
                for pair in range(2):
                    kinds = [(2 * pair + side - turn) % 4 for side in range(2)]
                    refs = [families[kind] for kind in kinds]
                    blocks = [
                        None if ref is None else ref[step // part_steps][step % part_steps]
                        for ref in refs
                    ]
                    start = (2 * step + pair) * lanes
                    for group in range(2):
                        part = slice(group * half, (group + 1) * half)
                        left_ref[group * rows : (group + 1) * rows, start : start + lanes] = (
                            jnp.concatenate(
                                [blank if x is None else x[:, part] for x in blocks], axis=1
                            )
                        )
            for step in range(0, steps, 2):
                cuts = []
                for inner in range(2):
                    start = (4 * (step + inner) + (turn + 2) % 4) * half
                    cuts.append(weight_ref[:, start : start + half])
                late_ref[:, step * half : (step + 2) * half] = jnp.concatenate(cuts, axis=1)

    wide = 256
    for start in range(0, hidden, wide):
        upper_ref[:, start : start + wide] = lax.dot_general(
            left_ref[...],
            weight_ref[start : start + wide, :],
            (((1,), (1,)), ((), ())),
            preferred_element_type=jnp.float32,
        )


def project_kernel(
    low_ref, high_ref, late_ref, upper_ref, h_two_ref, gate_ref, d_two_ref, part_ref,
    left_ref, sums_ref,
):
    steps, rows, lanes = low_ref.shape
    half = lanes // 2
    tokens, slots, wide = d_two_ref.shape
    own = slots // 2

    @pl.when(pl.program_id(0) == 0)
    def _():
        sums_ref[...] = jnp.zeros(sums_ref.shape, jnp.float32)
        for place, ref in enumerate((low_ref, high_ref)):
            for step in range(0, steps, 2):
                start = (place * steps + step) * half
                for group in range(2):
                    part = slice(group * half, (group + 1) * half)
                    left_ref[group * rows : (group + 1) * rows, start : start + lanes] = (
                        jnp.concatenate([ref[step][:, part], ref[step + 1][:, part]], axis=1)
                    )

    rest = lax.dot_general(
        left_ref[...], late_ref[...], (((1,), (1,)), ((), ())), preferred_element_type=jnp.float32
    )
    for group in range(2):
        keep = slice(group * own, (group + 1) * own)
        scale = gate_ref[keep, :][:, :1]
        total = sums_ref[keep, :]
        for pos in range(tokens):
            row = group * rows + pos * own
            piece = upper_ref[row : row + own, :] + rest[row : row + own, :]
            d_two_ref[pos, keep, :] = (piece * scale).astype(jnp.bfloat16)
            prod = h_two_ref[pos, keep, :].astype(jnp.float32) * piece
            for lane in range(0, wide, 128):
                total = total + prod[:, lane : lane + 128]
        sums_ref[keep, :] = total

    @pl.when(pl.program_id(0) == pl.num_programs(0) - 1)
    def _():
        row = lax.dot_general(
            jnp.ones((8, 128), jnp.float32),
            sums_ref[...],
            (((1,), (1,)), ((), ())),
            preferred_element_type=jnp.float32,
            precision=lax.Precision.HIGHEST,
        )[:1]
        part_ref[...] = jnp.broadcast_to(row[None], part_ref.shape)


def back_kernel(d_two_ref, slope_ref, taps_ref, kernel_ref, d_in_ref, d_one_ref, *, side):
    tokens, slots, hidden = d_two_ref.shape
    wide = 256
    for start in range(0, hidden, wide):
        span = slice(start, start + wide)
        for pos in range(tokens):
            total = jnp.zeros((slots, wide), jnp.float32)
            for off in range(9):
                other = near(pos, 8 - off, side)
                if other is not None:
                    total = total + d_two_ref[other, :, span].astype(jnp.float32) * taps_ref[
                        off : off + 1, span
                    ].astype(jnp.float32)
            d_one_ref[pos, :, span] = (total * slope_ref[pos, :, span]).astype(jnp.bfloat16)
    for pos in range(tokens):
        total = jnp.zeros(d_in_ref.shape[1:], jnp.float32)
        for off in range(9):
            other = near(pos, 8 - off, side)
            if other is not None:
                total = total + lax.dot_general(
                    d_one_ref[other],
                    kernel_ref[off],
                    (((1,), (1,)), ((), ())),
                    preferred_element_type=jnp.float32,
                )
        d_in_ref[pos] = total.astype(jnp.bfloat16)


def merge_kernel(parts_ref, d_in_ref, out_ref):
    tokens, slots, feat = d_in_ref.shape
    own = slots // 2
    totals = jnp.broadcast_to(jnp.sum(parts_ref[...], axis=0), (own, parts_ref.shape[2]))
    rows = lax.broadcasted_iota(jnp.int32, totals.shape, 0)
    cols = lax.broadcasted_iota(jnp.int32, totals.shape, 1)
    lines = []
    for pos in range(tokens):
        field = d_in_ref[pos].astype(jnp.float32)
        lines.append(jnp.concatenate([field[:own], field[own:]], axis=1))
    halves = []
    for group in range(2):
        mine = jnp.where(cols == rows + group * own, totals, 0.0)
        halves.append(jnp.broadcast_to(jnp.sum(mine, axis=1, keepdims=True), (own, feat)))
    lines.append(jnp.concatenate(halves, axis=1))
    while len(lines) < out_ref.shape[1]:
        lines.append(jnp.zeros_like(lines[0]))
    out_ref[...] = jnp.swapaxes(jnp.stack(lines), 0, 1).astype(jnp.bfloat16)


def finish_kernel(ids_ref, back_ref, grads_ref, gate_ref):
    tokens, owned, feat = grads_ref.shape
    sections = back_ref.shape[0]
    rows = lax.broadcasted_iota(jnp.int32, (owned, owned), 0)
    cols = lax.broadcasted_iota(jnp.int32, (owned, owned), 1)
    wide = jnp.broadcast_to(ids_ref[...], (owned, owned))
    column = jnp.sum(jnp.where(rows == cols, wide, 0), axis=1, keepdims=True)
    earlier = jnp.where((cols < rows) & (column == wide), 1, 0)
    rank = jnp.sum(earlier, axis=1, keepdims=True)
    named = column == lax.broadcasted_iota(jnp.int32, (owned, sections), 1)
    picks = [jnp.where(named & (rank == r), 1.0, 0.0).astype(jnp.bfloat16) for r in range(CAP)]
    lines = jnp.swapaxes(back_ref[...].astype(jnp.float32), 0, 1)

    def pick(line):
        line = line.astype(jnp.bfloat16)
        return jnp.dot(
            picks[0], line[:, :feat], preferred_element_type=jnp.float32
        ) + jnp.dot(picks[1], line[:, feat:], preferred_element_type=jnp.float32)

    for pos in range(tokens):
        grads_ref[pos] = pick(lines[pos]).astype(jnp.bfloat16)
    sums = jnp.broadcast_to(pick(lines[tokens])[:, :1], (owned, owned))
    sums = jnp.sum(jnp.where(rows == cols, sums, 0.0), axis=0, keepdims=True)
    gate_ref[...] = sums.astype(jnp.bfloat16)


def near_by(array):
    return pltpu.with_memory_space_constraint(array, pltpu.VMEM)


def vmem(count):
    return [pl.BlockSpec(memory_space=pltpu.VMEM) for _ in range(count)]


def on_device(tiles_in, grad_out, gate, expert_id, w_conv, w_depth, w_out):
    owned, side, _, feat = tiles_in.shape
    tokens = side * side
    sections = lax.axis_size("expert")
    slots = sections * CAP
    hidden = w_out.shape[1]
    group = w_conv.shape[3]

    def exchange(array):
        return lax.all_to_all(array, "expert", split_axis=0, concat_axis=0, tiled=True)

    lines = -(-(2 * tokens + 1) // 8) * 8
    outward = pl.pallas_call(
        prep_kernel,
        out_shape=jax.ShapeDtypeStruct((sections, lines, CAP * feat), jnp.bfloat16),
        in_specs=vmem(4),
        out_specs=vmem(1)[0],
        name="prep",
    )(
        expert_id.reshape(1, owned),
        gate.reshape(1, owned),
        grad_out.transpose(1, 2, 0, 3).reshape(tokens, owned, feat),
        tiles_in.transpose(1, 2, 0, 3).reshape(tokens, owned, feat),
    )
    arrived = exchange(outward)
    packed, inputs, gates = pl.pallas_call(
        sort_kernel,
        out_shape=(
            jax.ShapeDtypeStruct((tokens * sections, CAP * feat), jnp.bfloat16),
            jax.ShapeDtypeStruct((tokens, slots, feat), jnp.bfloat16),
            jax.ShapeDtypeStruct((slots, 128), jnp.float32),
        ),
        in_specs=vmem(1),
        out_specs=tuple(vmem(3)),
        compiler_params=pltpu.CompilerParams(vmem_limit_bytes=24 << 20),
        name="sort",
    )(near_by(arrived))
    chans = lax.axis_size("chan")
    steps = chans // 4
    families = [[4 * step + kind for step in range(steps)] for kind in range(4)]
    own = lax.all_gather(packed, "chan", axis=0, axis_index_groups=families)

    def shift(array, by):
        return lax.ppermute(array, "chan", [(c, (c + by) % chans) for c in range(chans)])

    part = jax.ShapeDtypeStruct((steps // 2, *own.shape[1:]), own.dtype)
    own_low, own_high = pl.pallas_call(
        split_kernel,
        out_shape=(part, part),
        in_specs=vmem(1),
        out_specs=tuple(vmem(2)),
        compiler_params=pltpu.CompilerParams(vmem_limit_bytes=24 << 20),
        name="split",
    )(near_by(own))
    prev_low = shift(own_low, 1)
    next_high = shift(own_high, -1)
    prev_high = shift(own_high, 1)
    next_low = shift(own_low, -1)
    low = shift(prev_low, 1)
    high = shift(next_high, -1)
    turn = (lax.axis_index("chan") % 4).astype(jnp.int32).reshape(1)

    taps = w_depth[0]
    small = w_conv[0].reshape(9, group, hidden)
    count = feat // group
    per = hidden // count
    which = jnp.arange(hidden, dtype=jnp.int32) // per
    kernel = jnp.concatenate(
        [jnp.where(which == g, small, jnp.zeros_like(small)) for g in range(count)], axis=1
    )
    h_two, slope = pl.pallas_call(
        lambda *refs: forward_kernel(*refs, side=side),
        out_shape=(
            jax.ShapeDtypeStruct((tokens, slots, hidden), jnp.bfloat16),
            jax.ShapeDtypeStruct((tokens, slots, hidden), jnp.float32),
        ),
        in_specs=vmem(3),
        out_specs=tuple(vmem(2)),
        scratch_shapes=[pltpu.VMEM((tokens, slots, hidden), jnp.float32)],
        compiler_params=pltpu.CompilerParams(vmem_limit_bytes=24 << 20),
        name="forward",
    )(inputs, kernel, taps)

    features = w_out.shape[2]
    upper, late = pl.pallas_call(
        early_kernel,
        out_shape=(
            jax.ShapeDtypeStruct((tokens * slots, hidden), jnp.float32),
            jax.ShapeDtypeStruct((hidden, features // 4), jnp.bfloat16),
        ),
        in_specs=[pl.BlockSpec(memory_space=pltpu.SMEM)] + vmem(7),
        out_specs=tuple(vmem(2)),
        scratch_shapes=[pltpu.VMEM((tokens * slots, features), jnp.bfloat16)],
        compiler_params=pltpu.CompilerParams(vmem_limit_bytes=24 << 20),
        name="early",
    )(
        turn,
        *[near_by(x) for x in (own_low, own_high, next_low, next_high, prev_low, prev_high)],
        near_by(w_out[0]),
    )
    wide = 256
    whole = lambda shape: pl.BlockSpec(shape, lambda i: (0,) * len(shape))
    d_two, part = pl.pallas_call(
        project_kernel,
        grid=(hidden // wide,),
        out_shape=(
            jax.ShapeDtypeStruct((tokens, slots, hidden), jnp.bfloat16),
            jax.ShapeDtypeStruct((chans, 1, 128), jnp.float32),
        ),
        in_specs=[
            whole(low.shape),
            whole(high.shape),
            pl.BlockSpec((wide, features // 4), lambda i: (i, 0)),
            pl.BlockSpec((tokens * slots, wide), lambda i: (0, i)),
            pl.BlockSpec((tokens, slots, wide), lambda i: (0, 0, i)),
            whole(gates.shape),
        ],
        out_specs=(
            pl.BlockSpec((tokens, slots, wide), lambda i: (0, 0, i)),
            whole((chans, 1, 128)),
        ),
        scratch_shapes=[
            pltpu.VMEM((tokens * slots, features // 4), jnp.bfloat16),
            pltpu.VMEM((128, 128), jnp.float32),
        ],
        compiler_params=pltpu.CompilerParams(vmem_limit_bytes=24 << 20),
        name="project",
    )(near_by(low), near_by(high), late, upper, h_two, gates)
    parts = lax.all_to_all(part, "chan", split_axis=0, concat_axis=0, tiled=True)
    d_input = pl.pallas_call(
        lambda *refs: back_kernel(*refs, side=side),
        out_shape=jax.ShapeDtypeStruct((tokens, slots, feat), jnp.bfloat16),
        in_specs=vmem(4),
        out_specs=vmem(1)[0],
        scratch_shapes=[pltpu.VMEM((tokens, slots, hidden), jnp.bfloat16)],
        compiler_params=pltpu.CompilerParams(vmem_limit_bytes=24 << 20),
        name="back",
    )(d_two, slope, taps, kernel)
    returned = -(-(tokens + 1) // 8) * 8
    limit = pltpu.CompilerParams(vmem_limit_bytes=24 << 20)
    back = pl.pallas_call(
        merge_kernel,
        out_shape=jax.ShapeDtypeStruct((sections, returned, CAP * feat), jnp.bfloat16),
        in_specs=vmem(2),
        out_specs=vmem(1)[0],
        compiler_params=limit,
        name="merge",
    )(near_by(parts), d_input)
    back = exchange(back)
    mine, mine_gate = pl.pallas_call(
        finish_kernel,
        out_shape=(
            jax.ShapeDtypeStruct((tokens, owned, feat), jnp.bfloat16),
            jax.ShapeDtypeStruct((1, owned), jnp.bfloat16),
        ),
        in_specs=vmem(2),
        out_specs=tuple(vmem(2)),
        compiler_params=limit,
        name="finish",
    )(expert_id.reshape(1, owned), near_by(back))
    mine = mine.reshape(side, side, owned, feat).transpose(2, 0, 1, 3)
    return (mine, mine_gate.reshape(owned))


def solution(mesh):
    in_specs = (
        P("expert", None, None, "chan"),
        P("expert", None, None, "chan"),
        P("expert"),
        P("expert", None),
        P("expert", None, None, None, "chan"),
        P("expert", None, "chan"),
        P("expert", "chan", None),
    )
    out_specs = (P("expert", None, None, "chan"), P("expert"))
    return jax.shard_map(
        on_device, mesh=mesh, in_specs=in_specs, out_specs=out_specs, check_vma=False
    )
```
